512 devices in a mesh: patch: 32 (over x, y), group: 16 (over z, core).
Axes of the slice: x: 4, y: 8, z: 8, core: 2. Of those that a mesh axis runs over, the one named last changes fastest.
Arguments:
- grid_latent: bfloat16 [262144, 512], P(('patch', 'group')), may hold values from -6 to 6
- mesh_latent: bfloat16 [131072, 512], P(('patch', 'group')), may hold values from -6 to 6
- cotangent: bfloat16 [131072, 512], P(('patch', 'group')), may hold values from -6 to 6
- halo_rows: int32 [131072], P(('patch', 'group')), may hold values from 0 to 511
- encoder_sender: int32 [393216], P(('patch', 'group')), may hold values from 0 to 767
- encoder_target: int32 [393216], P(('patch', 'group')), may hold values from 0 to 255
- encoder_count: int32 [512], P(('patch', 'group')), may hold values from 96 to 768, as said below
- process_sender: int32 [393216], P(('patch', 'group')), may hold values from 0 to 511
- process_target: int32 [393216], P(('patch', 'group')), may hold values from 0 to 255
- process_count: int32 [512], P(('patch', 'group')), may hold values from 96 to 768, as said below
- encoder_source: bfloat16 [512, 512], replicated, may hold values from -0.25 to 0.25
- encoder_dest: bfloat16 [512, 512], replicated, may hold values from -0.25 to 0.25
- encoder_output: bfloat16 [512, 512], replicated, may hold values from -0.25 to 0.25
- encoder_gain: float32 [512], replicated, may hold values from 0.5 to 1.5
- process_source: bfloat16 [512, 512], replicated, may hold values from -0.25 to 0.25
- process_dest: bfloat16 [512, 512], replicated, may hold values from -0.25 to 0.25
- process_output: bfloat16 [512, 512], replicated, may hold values from -0.25 to 0.25
- process_gain: float32 [512], replicated, may hold values from 0.5 to 1.5
Outputs:
- grid_grad: bfloat16 [262144, 512], P(('patch', 'group'))
- mesh_grad: bfloat16 [131072, 512], P(('patch', 'group'))
The draws below stay inside these ranges and needn't reach their ends.
Inputs may be any that keep to these rules, and one draw needn't show every extreme that they name: `halo_rows`: a block's entries are rows of its own grid nodes. `encoder_sender`: rows of the block's extended grid table. `encoder_target`: rows of the block's own mesh nodes. The first encoder_count slots of a block are edges, the rest padding; some block is full in every draw. `process_sender`: rows of the block's sender table: its own mesh nodes, then the coarse nodes of its group. `process_target`: rows of the block's own mesh nodes. The first process_count slots of a block are edges, the rest padding; some block is full in every draw.
All inputs are finite; a program needn't handle non-finite values.
Results may differ from the reference program's by a relative error of at most 0.01.
Values may be sent and summed in bfloat16 or wider, within the bound.
A program may use at most 64 MiB of HBM per device.

```python
import jax
import jax.numpy as jnp
from jax import lax

D = 512
HIDDEN_SIZE = 512
GRID_DEV = 512
MESH_DEV = 256
HALO = 128
COARSE_DEV = 16
E_CAP = 768
P_CAP = 768
GRID = 262144
MESH = 131072
N_PATCH = 32
N_GROUP = 16
DEVICES = 512


def draw_counts(key, capacity, salt_value):
    folded = jax.random.fold_in(key, salt_value)
    key_spread, key_full = jax.random.split(folded)
    spread = jax.random.randint(key_spread, (DEVICES,), 0, 64)
    floor_count = capacity // 8
    counts = floor_count + (capacity - floor_count) * spread * spread // 4096
    chosen = jax.random.randint(key_full, (), 0, DEVICES)
    return jnp.where(jnp.arange(DEVICES) == chosen, capacity, counts).astype(jnp.int32)


def draw_encoder_count(key, part):
    return draw_counts(key, E_CAP, 11)


def draw_process_count(key, part):
    return draw_counts(key, P_CAP, 23)


def place_ends(array, rng, smallest, high):
    longest = array.shape.index(max(array.shape))
    spots = []
    for shift in (0, 1):
        where = [jax.random.randint(jax.random.fold_in(rng, axis), (), 0, length) for axis, length in enumerate(array.shape)]
        where[longest] = (where[longest] + shift) % array.shape[longest]
        spots.append(tuple(where))
    return array.at[spots[0]].set(smallest).at[spots[1]].set(high)


def levels(key, dims, cuts, smallest, largest):
    def one(dim, parts):
        heights = jax.random.uniform(jax.random.fold_in(jax.random.fold_in(key, 6), dim), (parts,), jnp.float32, smallest / len(cuts), largest / len(cuts))
        return jnp.repeat(jnp.exp(heights), dims[dim] // parts).reshape((-1,) + (1,) * (len(dims) - dim - 1))

    level = one(*cuts[0])
    for cut in cuts[1:]:
        level = level * one(*cut)
    return level


def normal_values(rng, shape, scale, limit, cuts=(), kind=jnp.bfloat16):
    entries = scale * jax.random.normal(rng, shape, jnp.float32)
    if cuts:
        entries = entries * levels(rng, shape, cuts, -0.22, 0.18)
    return jnp.clip(entries, -limit, limit).astype(kind)


def setup_inputs(seed: int = 0) -> dict:
    keys = jax.random.split(jax.random.key(seed), 19)
    grid_latent = normal_values(keys[0], (GRID, D), 1.0, 6.0, ((0, 512),))
    mesh_latent = normal_values(keys[1], (MESH, D), 1.0, 6.0, ((0, 512),))
    cotangent = normal_values(keys[2], (MESH, D), 1.0, 6.0, ((0, 512),))
    halo_rows = place_ends(jax.random.randint(keys[3], (2 * HALO * DEVICES,), 0, GRID_DEV), jax.random.fold_in(keys[3], 1), 0, GRID_DEV - 1).astype(jnp.int32)
    encoder_sender = place_ends(jax.random.randint(keys[4], (E_CAP * DEVICES,), 0, GRID_DEV + 2 * HALO), jax.random.fold_in(keys[4], 1), 0, (GRID_DEV + 2 * HALO) - 1).astype(jnp.int32)
    encoder_target = place_ends(jax.random.randint(keys[5], (E_CAP * DEVICES,), 0, MESH_DEV), jax.random.fold_in(keys[5], 1), 0, MESH_DEV - 1).astype(jnp.int32)
    encoder_count = draw_encoder_count(jax.random.fold_in(keys[18], 71), 0)
    process_sender = place_ends(jax.random.randint(keys[7], (P_CAP * DEVICES,), 0, MESH_DEV + N_GROUP * COARSE_DEV), jax.random.fold_in(keys[7], 1), 0, (MESH_DEV + N_GROUP * COARSE_DEV) - 1).astype(jnp.int32)
    process_target = place_ends(jax.random.randint(keys[8], (P_CAP * DEVICES,), 0, MESH_DEV), jax.random.fold_in(keys[8], 1), 0, MESH_DEV - 1).astype(jnp.int32)
    process_count = draw_process_count(jax.random.fold_in(keys[18], 71), 0)
    encoder_source = normal_values(keys[10], (D, HIDDEN_SIZE), D ** -0.5, 0.25)
    encoder_dest = normal_values(keys[11], (D, HIDDEN_SIZE), D ** -0.5, 0.25)
    encoder_output = normal_values(keys[12], (HIDDEN_SIZE, D), HIDDEN_SIZE ** -0.5, 0.25)
    encoder_gain = jnp.clip(1.0 + 0.1 * jax.random.normal(keys[13], (D,), jnp.float32), 0.5, 1.5)
    process_source = normal_values(keys[14], (D, HIDDEN_SIZE), D ** -0.5, 0.25)
    process_dest = normal_values(keys[15], (D, HIDDEN_SIZE), D ** -0.5, 0.25)
    process_output = normal_values(keys[16], (HIDDEN_SIZE, D), HIDDEN_SIZE ** -0.5, 0.25)
    process_gain = jnp.clip(1.0 + 0.1 * jax.random.normal(keys[17], (D,), jnp.float32), 0.5, 1.5)
    return dict(grid_latent=grid_latent, mesh_latent=mesh_latent, cotangent=cotangent, halo_rows=halo_rows, encoder_sender=encoder_sender, encoder_target=encoder_target, encoder_count=encoder_count, process_sender=process_sender, process_target=process_target, process_count=process_count, encoder_source=encoder_source, encoder_dest=encoder_dest, encoder_output=encoder_output, encoder_gain=encoder_gain, process_source=process_source, process_dest=process_dest, process_output=process_output, process_gain=process_gain)


EPSILON = 1e-05

def silu_slope(values):
    logistic = jax.nn.sigmoid(values)
    return logistic * (1.0 + values * (1.0 - logistic))

def norm_forward(values, norm_gain):
    center = values - lax.optimization_barrier(jnp.mean(values, axis=-1, keepdims=True))
    inverse = lax.rsqrt(lax.optimization_barrier(jnp.mean(center * center, axis=-1, keepdims=True)) + EPSILON)
    normed = center * inverse
    return (normed * norm_gain, normed, inverse)

def norm_backward(grad_out, normed, inverse, norm_gain):
    scaled = grad_out * norm_gain
    return inverse * (scaled - lax.optimization_barrier(jnp.mean(scaled, axis=-1, keepdims=True)) - normed * lax.optimization_barrier(jnp.mean(scaled * normed, axis=-1, keepdims=True)))

def edge_forward(source, dest_proj, sender, target, live_count, out_weight, mesh_count):
    preact = source[sender] + dest_proj[target]
    hidden = jax.nn.silu(preact).astype(jnp.bfloat16)
    message = jnp.dot(hidden, out_weight, preferred_element_type=jnp.float32).astype(jnp.bfloat16)
    live_slots = jnp.arange(sender.shape[0], dtype=jnp.int32) < live_count
    onehot = ((target[None, :] == jnp.arange(mesh_count, dtype=jnp.int32)[:, None]) & live_slots[None, :]).astype(jnp.bfloat16)
    gathered = jnp.dot(onehot, message, preferred_element_type=jnp.float32)
    return (gathered, preact, onehot, live_slots)

def edge_backward(grad_gathered, preact, onehot, live_slots, sender, target, out_weight, table_rows):
    grad_message = jnp.where(live_slots[:, None], grad_gathered[target], 0.0).astype(jnp.bfloat16)
    grad_hidden = jnp.dot(grad_message, out_weight.T, preferred_element_type=jnp.float32)
    grad_preact = (grad_hidden * silu_slope(preact)).astype(jnp.bfloat16)
    chooser = (sender[None, :] == jnp.arange(table_rows, dtype=jnp.int32)[:, None]).astype(jnp.bfloat16)
    grad_source = jnp.dot(chooser, grad_preact, preferred_element_type=jnp.float32)
    grad_dest = jnp.dot(onehot, grad_preact, preferred_element_type=jnp.float32)
    return (grad_source, grad_dest)

def encoder_pass(extended, mesh_rows, sender, target, live_count, source_weight, dest_weight, out_weight, norm_gain):
    source = jnp.dot(extended, source_weight, preferred_element_type=jnp.float32)
    dest_proj = jnp.dot(mesh_rows, dest_weight, preferred_element_type=jnp.float32)
    gathered, preact, onehot, live_slots = edge_forward(source, dest_proj, sender, target, live_count, out_weight, mesh_rows.shape[0])
    shifted, normed, inverse = norm_forward(gathered, norm_gain)
    updated = (mesh_rows.astype(jnp.float32) + shifted).astype(jnp.bfloat16)
    return (updated, (preact, onehot, live_slots, normed, inverse))

def encoder_backward(grad_updated, stored, table_rows, sender, target, source_weight, dest_weight, out_weight, norm_gain):
    preact, onehot, live_slots, normed, inverse = stored
    grad_gathered = norm_backward(grad_updated, normed, inverse, norm_gain)
    grad_source, grad_dest = edge_backward(grad_gathered, preact, onehot, live_slots, sender, target, out_weight, table_rows)
    mesh_grad = grad_updated + jnp.dot(grad_dest.astype(jnp.bfloat16), dest_weight.T, preferred_element_type=jnp.float32)
    grad_extended = jnp.dot(grad_source.astype(jnp.bfloat16), source_weight.T, preferred_element_type=jnp.float32)
    return (mesh_grad, grad_extended)

def process_grads(updated, coarse_proj, sender, target, live_count, cotangent, source_weight, dest_weight, out_weight, norm_gain):
    local_proj = jnp.dot(updated, source_weight, preferred_element_type=jnp.float32)
    source = jnp.concatenate([local_proj, coarse_proj], axis=0)
    dest_proj = jnp.dot(updated, dest_weight, preferred_element_type=jnp.float32)
    gathered, preact, onehot, live_slots = edge_forward(source, dest_proj, sender, target, live_count, out_weight, updated.shape[0])
    unused, normed, inverse = norm_forward(gathered, norm_gain)
    grad_out = cotangent.astype(jnp.float32)
    grad_gathered = norm_backward(grad_out, normed, inverse, norm_gain)
    grad_source, grad_dest = edge_backward(grad_gathered, preact, onehot, live_slots, sender, target, out_weight, source.shape[0])
    mesh_count = updated.shape[0]
    grad_local = grad_out + jnp.dot(grad_source[:mesh_count].astype(jnp.bfloat16), source_weight.T, preferred_element_type=jnp.float32)
    grad_local = grad_local + jnp.dot(grad_dest.astype(jnp.bfloat16), dest_weight.T, preferred_element_type=jnp.float32)
    return (grad_local, grad_source[mesh_count:])

def add_rim(base_rows, rim_index, returned):
    return base_rows.at[rim_index].add(returned)

def reference(grid_latent, mesh_latent, cotangent, halo_rows, encoder_sender, encoder_target, encoder_count, process_sender, process_target, process_count, encoder_source, encoder_dest, encoder_output, encoder_gain, process_source, process_dest, process_output, process_gain):
    blocks = N_PATCH * N_GROUP
    grid_blocks = grid_latent.reshape(blocks, GRID_DEV, D)
    mesh_blocks = mesh_latent.reshape(blocks, MESH_DEV, D)
    cotangents = cotangent.reshape(blocks, MESH_DEV, D)
    rim_index = halo_rows.reshape(blocks, 2 * HALO)
    outgoing = jnp.take_along_axis(grid_blocks, rim_index[:, :, None], axis=1)
    by_patch = outgoing.reshape(N_PATCH, N_GROUP, 2 * HALO, D)
    from_before = jnp.roll(by_patch, 1, axis=0)[:, :, HALO:].reshape(blocks, HALO, D)
    from_after = jnp.roll(by_patch, -1, axis=0)[:, :, :HALO].reshape(blocks, HALO, D)
    extended = jnp.concatenate([grid_blocks, from_before, from_after], axis=1)
    enc_senders = encoder_sender.reshape(blocks, E_CAP)
    enc_targets = encoder_target.reshape(blocks, E_CAP)
    proc_senders = process_sender.reshape(blocks, P_CAP)
    proc_targets = process_target.reshape(blocks, P_CAP)

    def encode_block(pieces):
        table, mesh_rows, sender, target, live_count = pieces
        return encoder_pass(table, mesh_rows, sender, target, live_count, encoder_source, encoder_dest, encoder_output, encoder_gain)[0]
    updated = lax.map(encode_block, (extended, mesh_blocks, enc_senders, enc_targets, encoder_count))
    coarse = updated.reshape(N_PATCH, N_GROUP, MESH_DEV, D)[:, :, :COARSE_DEV].reshape(N_PATCH * N_GROUP * COARSE_DEV, D)
    coarse_proj = jnp.dot(coarse, process_source, preferred_element_type=jnp.float32).reshape(N_PATCH, N_GROUP * COARSE_DEV, HIDDEN_SIZE)

    def process_block(pieces):
        number, mesh_rows, sender, target, live_count, cot_rows = pieces
        return process_grads(mesh_rows, coarse_proj[number // N_GROUP], sender, target, live_count, cot_rows, process_source, process_dest, process_output, process_gain)
    numbers = jnp.arange(blocks, dtype=jnp.int32)
    grad_local, grad_coarse = lax.map(process_block, (numbers, updated, proc_senders, proc_targets, process_count, cotangents))
    summed = lax.optimization_barrier(jnp.sum(grad_coarse.reshape(N_PATCH, N_GROUP, N_GROUP * COARSE_DEV, HIDDEN_SIZE), axis=1))
    summed = summed.reshape(blocks * COARSE_DEV, HIDDEN_SIZE)
    back_weight = process_source.astype(jnp.float32).T
    coarse_grad = jnp.dot(summed, back_weight, precision=lax.Precision.HIGHEST, preferred_element_type=jnp.float32)
    grad_updated = grad_local.at[:, :COARSE_DEV].add(coarse_grad.reshape(blocks, COARSE_DEV, D))

    def encode_back(pieces):
        grad_rows, table, mesh_rows, sender, target, live_count = pieces
        unused, stored = encoder_pass(table, mesh_rows, sender, target, live_count, encoder_source, encoder_dest, encoder_output, encoder_gain)
        return encoder_backward(grad_rows, stored, table.shape[0], sender, target, encoder_source, encoder_dest, encoder_output, encoder_gain)
    mesh_grad, grad_extended = lax.map(encode_back, (grad_updated, extended, mesh_blocks, enc_senders, enc_targets, encoder_count))
    grad_before = grad_extended[:, GRID_DEV:GRID_DEV + HALO].reshape(N_PATCH, N_GROUP, HALO, D)
    grad_after = grad_extended[:, GRID_DEV + HALO:].reshape(N_PATCH, N_GROUP, HALO, D)
    returned = jnp.concatenate([jnp.roll(grad_after, 1, axis=0), jnp.roll(grad_before, -1, axis=0)], axis=2)
    returned = returned.reshape(blocks, 2 * HALO, D)
    grid_grad = jax.vmap(add_rim)(grad_extended[:, :GRID_DEV], rim_index, returned)
    return (grid_grad.reshape(GRID, D).astype(jnp.bfloat16), mesh_grad.reshape(MESH, D).astype(jnp.bfloat16))
```

```python
import functools

import jax
import jax.numpy as jnp
from jax import lax
from jax.experimental import pallas as pl
from jax.experimental.pallas import tpu as pltpu
from jax.sharding import PartitionSpec as P

EPSILON = 1e-05
F32 = jnp.float32
BF16 = jnp.bfloat16
COARSE = 16
LANES = 128


def mm(a, b):
    return jnp.dot(a, b, preferred_element_type=F32)


def mm_t(a, b):
    return lax.dot_general(a, b, (((1,), (1,)), ((), ())), preferred_element_type=F32)


def column(row):
    return jnp.transpose(jnp.broadcast_to(row, (LANES, row.shape[1])))


def onehot_cols(ref, col, start, stop, shift):
    lane = lax.broadcasted_iota(jnp.int32, (col.shape[0], LANES), 1)
    for c in range(start, stop, LANES):
        width = min(LANES, stop - c)
        hit = jnp.where(col == lane + (c - shift), 1.0, 0.0).astype(BF16)
        ref[:, c : c + width] = hit[:, :width]


def onehot_rows(ref, row, start, stop, shift):
    for c in range(start, stop, LANES):
        height = min(LANES, stop - c)
        sub = lax.broadcasted_iota(jnp.int32, (height, row.shape[1]), 0)
        hit = jnp.where(row == sub + (c - shift), 1.0, 0.0).astype(BF16)
        ref[c : c + height, :] = hit


def norm_backward(scaled, normed, inverse):
    first = jnp.mean(scaled, axis=-1, keepdims=True)
    second = jnp.mean(scaled * normed, axis=-1, keepdims=True)
    return inverse * (scaled - first - normed * second)


def norm_forward(values):
    center = values - jnp.mean(values, axis=-1, keepdims=True)
    inverse = lax.rsqrt(jnp.mean(center * center, axis=-1, keepdims=True) + EPSILON)
    return center * inverse, inverse


def silu_pair(values):
    logistic = 0.5 * jnp.tanh(0.5 * values) + 0.5
    hidden = values * logistic
    return hidden, logistic + hidden * (1.0 - logistic)


def kernel(
    n_patch,
    n_group,
    grid_hbm,
    mesh_hbm,
    cot_hbm,
    w_src_hbm,
    w_dst_hbm,
    w_out_hbm,
    p_src_hbm,
    p_dst_hbm,
    p_out_hbm,
    halo_ref,
    e_send_ref,
    e_targ_ref,
    e_count_ref,
    p_send_ref,
    p_targ_ref,
    p_count_ref,
    e_gain_ref,
    p_gain_ref,
    grid_out,
    mesh_out,
    ext,
    mesh_v,
    cot_v,
    w_src,
    w_dst,
    w_out,
    p_src,
    p_dst,
    p_out,
    outgoing,
    hot_h,
    hot_ht,
    hot1,
    hot1t,
    hot2,
    hot2t,
    tbl1,
    tbl2,
    coarse,
    acc,
    slope1,
    slope2,
    hid,
    gpre,
    normed,
    inv,
    gup,
    gnode,
    gnode16,
    gcoarse,
    rs_buf,
    g_halo,
    peers,
    own,
    load_sem,
    halo_send,
    halo_recv,
    co_send,
    co_recv,
    rs_send,
    rs_recv,
    back_send,
    back_recv,
):
    patch, group = lax.axis_index("patch"), lax.axis_index("group")
    after = lax.rem(patch + 1, n_patch)
    before = lax.rem(patch + n_patch - 1, n_patch)
    grid_rows, mesh_rows = grid_hbm.shape[0], mesh_hbm.shape[0]
    rim = outgoing.shape[0] // 2
    slots = e_send_ref.shape[1]
    chunk = 256
    mesh_id = pl.DeviceIdType.MESH

    loads = []
    pairs = (
        (grid_hbm, ext.at[0:grid_rows]),
        (w_src_hbm, w_src),
        (mesh_hbm, mesh_v),
        (w_dst_hbm, w_dst),
        (w_out_hbm, w_out),
        (p_src_hbm, p_src),
        (p_dst_hbm, p_dst),
        (p_out_hbm, p_out),
        (cot_hbm, cot_v),
    )
    for n, (src, dst) in enumerate(pairs):
        copy = pltpu.make_async_copy(src, dst, load_sem.at[n])
        copy.start()
        loads.append(copy)

    barrier = pltpu.get_barrier_semaphore()
    for neighbour in (before, after):
        pl.semaphore_signal(
            barrier, inc=1, device_id={"patch": neighbour}, device_id_type=mesh_id
        )

    def greet(k, carry):
        peer = lax.rem(group + k, n_group)
        pl.semaphore_signal(barrier, inc=1, device_id={"group": peer}, device_id_type=mesh_id)
        return carry

    lax.fori_loop(1, n_group, greet, 0)

    halo_row = halo_ref[...]
    onehot_cols(hot_h, column(halo_row), 0, grid_rows, 0)
    loads[0].wait()
    outgoing[...] = mm(hot_h[...], ext[0:grid_rows, :]).astype(BF16)
    pl.semaphore_wait(barrier, n_group + 1)

    def remote(src, dst, send, recv, where):
        return pltpu.make_async_remote_copy(
            src_ref=src,
            dst_ref=dst,
            send_sem=send,
            recv_sem=recv,
            device_id=where,
            device_id_type=mesh_id,
        )

    up = remote(
        outgoing.at[rim : 2 * rim],
        ext.at[grid_rows : grid_rows + rim],
        halo_send.at[0],
        halo_recv.at[0],
        {"patch": after},
    )
    down = remote(
        outgoing.at[0:rim],
        ext.at[grid_rows + rim : grid_rows + 2 * rim],
        halo_send.at[1],
        halo_recv.at[1],
        {"patch": before},
    )
    up.start()
    down.start()

    slot = lax.broadcasted_iota(jnp.int32, (1, slots), 1)
    own1 = grid_rows + mesh_rows
    sender = e_send_ref[...]
    sender = jnp.where(sender >= grid_rows, sender + mesh_rows, sender)
    target = jnp.where(slot < e_count_ref[0], e_targ_ref[...], -1)
    sender_col, target_col = column(sender), column(target)
    onehot_cols(hot1, sender_col, 0, grid_rows, 0)
    onehot_cols(hot1, target_col, grid_rows, own1, grid_rows)
    onehot_cols(hot1, sender_col, own1, own1 + 2 * rim, 0)
    loads[1].wait()
    tbl1[0:grid_rows, :] = mm(ext[0:grid_rows, :], w_src[...]).astype(BF16)
    loads[2].wait()
    loads[3].wait()
    tbl1[grid_rows:own1, :] = mm(mesh_v[...], w_dst[...]).astype(BF16)

    def chunks(body):
        def step(i, carry):
            body(pl.ds(pl.multiple_of(i * chunk, chunk), chunk))
            return carry

        lax.fori_loop(0, slots // chunk, step, 0)

    def early1(rows):
        acc[rows, :] = mm(hot1[rows, 0:own1], tbl1[0:own1, :])

    chunks(early1)
    onehot_rows(hot1t, sender, 0, grid_rows, 0)
    onehot_rows(hot1t, target, grid_rows, own1, grid_rows)
    onehot_rows(hot1t, sender, own1, own1 + 2 * rim, 0)
    p_sender = p_send_ref[...]
    p_sender = jnp.where(p_sender >= mesh_rows, p_sender + mesh_rows, p_sender)
    p_target = jnp.where(slot < p_count_ref[0], p_targ_ref[...], -1)
    p_sender_col, p_target_col = column(p_sender), column(p_target)
    local2 = 2 * mesh_rows
    all2 = local2 + coarse.shape[0]
    onehot_cols(hot2, p_sender_col, 0, mesh_rows, 0)
    onehot_cols(hot2, p_target_col, mesh_rows, local2, mesh_rows)
    onehot_cols(hot2, p_sender_col, local2, all2, 0)
    onehot_rows(hot2t, p_sender, 0, mesh_rows, 0)
    onehot_rows(hot2t, p_target, mesh_rows, local2, mesh_rows)
    onehot_rows(hot2t, p_sender, local2, all2, 0)
    onehot_rows(hot_ht, halo_row, 0, grid_rows, 0)

    up.wait()
    down.wait()
    tbl1[own1 : own1 + 2 * rim, :] = mm(ext[grid_rows : grid_rows + 2 * rim, :], w_src[...]).astype(
        BF16
    )

    def late1(rows):
        preact = acc[rows, :] + mm(hot1[rows, own1 : own1 + 2 * rim], tbl1[own1 : own1 + 2 * rim, :])
        hidden, slope = silu_pair(preact)
        hid[rows, :] = hidden.astype(BF16)
        slope1[rows, :] = slope

    chunks(late1)
    for n in range(4, len(pairs)):
        loads[n].wait()
    summed = mm(hot1t[grid_rows:own1, :], hid[...]).astype(BF16)
    normed1, inverse1 = norm_forward(mm(summed, w_out[...]))
    normed[...] = normed1
    inv[...] = jnp.broadcast_to(inverse1, inv.shape)
    updated = (mesh_v[...].astype(F32) + normed1 * e_gain_ref[...]).astype(BF16)
    projected = mm(updated, p_src[...]).astype(BF16)
    tbl2[0:mesh_rows, :] = projected
    own_rows = pl.ds(pl.multiple_of(group * COARSE, COARSE), COARSE)

    def coarse_copy(k):
        return remote(
            tbl2.at[0:COARSE],
            coarse.at[own_rows],
            co_send.at[k - 1],
            co_recv.at[k - 1],
            {"group": lax.rem(group + k, n_group)},
        )

    def each_peer(body):
        def step(k, carry):
            body(k)
            return carry

        lax.fori_loop(1, n_group, step, 0)

    each_peer(lambda k: coarse_copy(k).start())
    coarse[own_rows, :] = projected[0:COARSE, :]
    tbl2[mesh_rows:local2, :] = mm(updated, p_dst[...]).astype(BF16)

    def early2(rows):
        acc[rows, :] = mm(hot2[rows, 0:local2], tbl2[...])

    chunks(early2)
    each_peer(lambda k: coarse_copy(k).wait())

    def late2(rows):
        preact = acc[rows, :] + mm(hot2[rows, local2:all2], coarse[...])
        hidden, slope = silu_pair(preact)
        hid[rows, :] = hidden.astype(BF16)
        slope2[rows, :] = slope

    chunks(late2)
    summed2 = mm(hot2t[mesh_rows:local2, :], hid[...]).astype(BF16)
    normed2, inverse2 = norm_forward(mm(summed2, p_out[...]))
    cot = cot_v[...].astype(F32)
    node2 = norm_backward(cot * p_gain_ref[...], normed2, inverse2).astype(BF16)
    gnode[...] = mm_t(node2, p_out[...]).astype(BF16)

    def back2(rows):
        grad = mm(hot2[rows, mesh_rows:local2], gnode[...])
        gpre[rows, :] = (grad * slope2[rows, :]).astype(BF16)

    chunks(back2)
    gcoarse[...] = mm(hot2t[local2:all2, :], gpre[...]).astype(BF16)

    def rs_copy(k):
        peer = lax.rem(group + k, n_group)
        return remote(
            gcoarse.at[pl.ds(pl.multiple_of(peer * COARSE, COARSE), COARSE)],
            rs_buf.at[k - 1],
            rs_send.at[k - 1],
            rs_recv.at[k - 1],
            {"group": peer},
        )

    each_peer(lambda k: rs_copy(k).start())
    g_local = mm(hot2t[0:mesh_rows, :], gpre[...]).astype(BF16)
    g_dest = mm(hot2t[mesh_rows:local2, :], gpre[...]).astype(BF16)
    grad_up = cot + mm_t(g_local, p_src[...]) + mm_t(g_dest, p_dst[...])
    gup[...] = grad_up
    gain = e_gain_ref[...]
    node1 = norm_backward(grad_up * gain, normed[...], inv[:, 0:1])
    row = lax.broadcasted_iota(jnp.int32, node1.shape, 0)
    node1 = jnp.where(row < COARSE, 0.0, node1).astype(BF16)
    gnode[...] = mm_t(node1, w_out[...]).astype(BF16)

    def early3(rows):
        acc[rows, :] = mm(hot1[rows, grid_rows:own1], gnode[...])

    chunks(early3)
    gnode16[...] = jnp.zeros_like(gnode16)
    each_peer(lambda k: rs_copy(k).wait())

    total = gcoarse[own_rows, :].astype(F32)
    for k in range(n_group - 1):
        total = total + rs_buf[k].astype(F32)
    high = total.astype(BF16)
    low = (total - high.astype(F32)).astype(BF16)
    both = mm_t(jnp.concatenate([high, low], axis=0), p_src[...])
    fixed = gup[0:COARSE, :] + both[0:COARSE, :] + both[COARSE:, :]
    gup[0:COARSE, :] = fixed
    node16 = norm_backward(fixed * gain, normed[0:COARSE, :], inv[0:COARSE, 0:1]).astype(BF16)
    gnode16[0:COARSE, :] = mm_t(node16, w_out[...]).astype(BF16)

    def late3(rows):
        grad = acc[rows, :] + mm(hot1[rows, grid_rows : grid_rows + LANES], gnode16[...])
        gpre[rows, :] = (grad * slope1[rows, :]).astype(BF16)

    chunks(late3)
    g_halo[...] = mm(hot1t[own1 : own1 + 2 * rim, :], gpre[...]).astype(BF16)
    back_up = remote(
        g_halo.at[rim : 2 * rim],
        peers.at[0:rim],
        back_send.at[0],
        back_recv.at[0],
        {"patch": after},
    )
    back_down = remote(
        g_halo.at[0:rim],
        peers.at[rim : 2 * rim],
        back_send.at[1],
        back_recv.at[1],
        {"patch": before},
    )
    back_up.start()
    back_down.start()
    g_own = mm(hot1t[0:grid_rows, :], gpre[...]).astype(BF16)
    own[...] = mm_t(g_own, w_src[...])
    g_targ = mm(hot1t[grid_rows:own1, :], gpre[...]).astype(BF16)
    mesh_out[...] = (gup[...] + mm_t(g_targ, w_dst[...])).astype(BF16)
    back_up.wait()
    back_down.wait()
    returned = mm_t(peers[...], w_src[...]).astype(BF16)
    grid_out[...] = (own[...] + mm(hot_ht[...], returned)).astype(BF16)


def on_device(
    n_patch,
    n_group,
    grid_latent,
    mesh_latent,
    cotangent,
    halo_rows,
    encoder_sender,
    encoder_target,
    encoder_count,
    process_sender,
    process_target,
    process_count,
    encoder_source,
    encoder_dest,
    encoder_output,
    encoder_gain,
    process_source,
    process_dest,
    process_output,
    process_gain,
):
    g, d = grid_latent.shape
    m = mesh_latent.shape[0]
    h2 = halo_rows.shape[0]
    e = encoder_sender.shape[0]
    nc = n_group * COARSE
    hbm = pl.BlockSpec(memory_space=pl.ANY)
    vmem = pl.BlockSpec(memory_space=pltpu.VMEM)
    smem = pl.BlockSpec(memory_space=pltpu.SMEM)
    dma = pltpu.SemaphoreType.DMA
    out = pl.pallas_call(
        functools.partial(kernel, n_patch, n_group),
        out_shape=(
            jax.ShapeDtypeStruct((g, d), BF16),
            jax.ShapeDtypeStruct((m, d), BF16),
        ),
        in_specs=[hbm] * 9 + [vmem, vmem, vmem, smem, vmem, vmem, smem, vmem, vmem],
        out_specs=(vmem, vmem),
        scratch_shapes=[
            pltpu.VMEM((g + h2, d), BF16),
            pltpu.VMEM((m, d), BF16),
            pltpu.VMEM((m, d), BF16),
        ]
        + [pltpu.VMEM((d, d), BF16)] * 6
        + [
            pltpu.VMEM((h2, d), BF16),
            pltpu.VMEM((h2, g), BF16),
            pltpu.VMEM((g, h2), BF16),
            pltpu.VMEM((e, g + m + h2), BF16),
            pltpu.VMEM((g + m + h2, e), BF16),
            pltpu.VMEM((e, 2 * m + nc), BF16),
            pltpu.VMEM((2 * m + nc, e), BF16),
            pltpu.VMEM((g + m + h2, d), BF16),
            pltpu.VMEM((2 * m, d), BF16),
            pltpu.VMEM((nc, d), BF16),
            pltpu.VMEM((e, d), F32),
            pltpu.VMEM((e, d), F32),
            pltpu.VMEM((e, d), F32),
            pltpu.VMEM((e, d), BF16),
            pltpu.VMEM((e, d), BF16),
            pltpu.VMEM((m, d), F32),
            pltpu.VMEM((m, LANES), F32),
            pltpu.VMEM((m, d), F32),
            pltpu.VMEM((m, d), BF16),
            pltpu.VMEM((LANES, d), BF16),
            pltpu.VMEM((nc, d), BF16),
            pltpu.VMEM((n_group - 1, COARSE, d), BF16),
            pltpu.VMEM((h2, d), BF16),
            pltpu.VMEM((h2, d), BF16),
            pltpu.VMEM((g, d), F32),
            dma((9,)),
            dma((2,)),
            dma((2,)),
            dma((n_group - 1,)),
            dma((n_group - 1,)),
            dma((n_group - 1,)),
            dma((n_group - 1,)),
            dma((2,)),
            dma((2,)),
        ],
        compiler_params=pltpu.CompilerParams(
            collective_id=0, has_side_effects=True, vmem_limit_bytes=40 * 1024 * 1024
        ),
        name="step",
    )(
        grid_latent,
        mesh_latent,
        cotangent,
        encoder_source,
        encoder_dest,
        encoder_output,
        process_source,
        process_dest,
        process_output,
        halo_rows.reshape(1, h2),
        encoder_sender.reshape(1, e),
        encoder_target.reshape(1, e),
        encoder_count,
        process_sender.reshape(1, e),
        process_target.reshape(1, e),
        process_count,
        encoder_gain.reshape(1, d),
        process_gain.reshape(1, d),
    )
    return out


def solution(mesh):
    both = P(("patch", "group"))
    rows = P(("patch", "group"), None)
    return jax.shard_map(
        functools.partial(on_device, mesh.shape["patch"], mesh.shape["group"]),
        mesh=mesh,
        in_specs=(rows,) * 3 + (both,) * 7 + (P(),) * 8,
        out_specs=(rows, rows),
        check_vma=False,
    )
```

```python
import functools

import jax
import jax.numpy as jnp
from jax import lax
from jax.experimental import pallas as pl
from jax.experimental.pallas import tpu as pltpu
from jax.sharding import PartitionSpec as P

EPSILON = 1e-05
F32 = jnp.float32
BF16 = jnp.bfloat16
COARSE = 16
LANES = 128


def mm(a, b):
    return jnp.dot(a, b, preferred_element_type=F32)


def mm_t(a, b):
    return lax.dot_general(a, b, (((1,), (1,)), ((), ())), preferred_element_type=F32)


def column(row):
    return jnp.transpose(jnp.broadcast_to(row, (LANES, row.shape[1])))


def onehot_cols(ref, col, start, stop, shift):
    lane = lax.broadcasted_iota(jnp.int32, (col.shape[0], LANES), 1)
    for c in range(start, stop, LANES):
        width = min(LANES, stop - c)
        hit = jnp.where(col == lane + (c - shift), 1.0, 0.0).astype(BF16)
        ref[:, c : c + width] = hit[:, :width]


def onehot_rows(ref, row, start, stop, shift):
    for c in range(start, stop, LANES):
        height = min(LANES, stop - c)
        sub = lax.broadcasted_iota(jnp.int32, (height, row.shape[1]), 0)
        hit = jnp.where(row == sub + (c - shift), 1.0, 0.0).astype(BF16)
        ref[c : c + height, :] = hit


def norm_backward(scaled, normed, inverse):
    first = jnp.mean(scaled, axis=-1, keepdims=True)
    second = jnp.mean(scaled * normed, axis=-1, keepdims=True)
    return inverse * (scaled - first - normed * second)


def norm_forward(values):
    center = values - jnp.mean(values, axis=-1, keepdims=True)
    inverse = lax.rsqrt(jnp.mean(center * center, axis=-1, keepdims=True) + EPSILON)
    return center * inverse, inverse


def silu_pair(values):
    logistic = 0.5 * jnp.tanh(0.5 * values) + 0.5
    hidden = values * logistic
    return hidden, logistic + hidden * (1.0 - logistic)


def silu(values):
    return values * (0.5 * jnp.tanh(0.5 * values) + 0.5)


def kernel(
    n_patch,
    n_group,
    grid_hbm,
    mesh_hbm,
    cot_hbm,
    w_src_hbm,
    w_dst_hbm,
    w_out_hbm,
    p_src_hbm,
    p_dst_hbm,
    p_out_hbm,
    halo_hbm,
    e_send_hbm,
    e_targ_hbm,
    e_count_ref,
    p_send_hbm,
    p_targ_hbm,
    p_count_ref,
    e_gain_hbm,
    p_gain_hbm,
    grid_out,
    mesh_out,
    ext,
    mesh_v,
    cot_v,
    w_src,
    w_dst,
    w_out,
    p_src,
    p_dst,
    p_out,
    outgoing,
    hot_h,
    hot_ht,
    hot1,
    hot1t,
    hot2,
    hot2t,
    tbl1,
    tbl2,
    coarse,
    acc,
    slope1,
    slope2,
    hid,
    gpre,
    normed,
    inv,
    gup,
    gnode,
    gnode16,
    gcoarse,
    rs_buf,
    g_halo,
    peers,
    own,
    halo_ref,
    e_send_ref,
    e_targ_ref,
    p_send_ref,
    p_targ_ref,
    e_gain_ref,
    p_gain_ref,
    load_sem,
    halo_send,
    halo_recv,
    co_send,
    co_recv,
    swap_sem,
    rs_send,
    rs_recv,
    back_send,
    back_recv,
):
    patch, group = lax.axis_index("patch"), lax.axis_index("group")
    after = lax.rem(patch + 1, n_patch)
    before = lax.rem(patch + n_patch - 1, n_patch)
    grid_rows, mesh_rows = grid_hbm.shape[0], mesh_hbm.shape[0]
    rim = outgoing.shape[0] // 2
    slots = e_send_ref.shape[0]
    chunk = 256
    mesh_id = pl.DeviceIdType.MESH

    pairs = (
        (halo_hbm, halo_ref),
        (grid_hbm, ext.at[0:grid_rows]),
        (e_send_hbm, e_send_ref),
        (e_targ_hbm, e_targ_ref),
        (w_src_hbm, w_src),
        (mesh_hbm, mesh_v),
        (w_dst_hbm, w_dst),
        (p_send_hbm, p_send_ref),
        (p_targ_hbm, p_targ_ref),
        (e_gain_hbm, e_gain_ref),
        (p_gain_hbm, p_gain_ref),
        (w_out_hbm, w_out),
        (p_src_hbm, p_src),
        (p_dst_hbm, p_dst),
        (p_out_hbm, p_out),
        (cot_hbm, cot_v),
    )
    loads = [
        pltpu.make_async_copy(src, dst, load_sem.at[n]) for n, (src, dst) in enumerate(pairs)
    ]
    for n in range(5):
        loads[n].start()

    barrier = pltpu.get_barrier_semaphore()
    for neighbour in (before, after):
        pl.semaphore_signal(
            barrier, inc=1, device_id={"patch": neighbour}, device_id_type=mesh_id
        )

    def greet(k, carry):
        peer = lax.rem(group + k, n_group)
        pl.semaphore_signal(barrier, inc=1, device_id={"group": peer}, device_id_type=mesh_id)
        return carry

    lax.fori_loop(1, n_group, greet, 0)

    loads[0].wait()
    halo_row = halo_ref[...].reshape(1, 2 * rim)
    onehot_cols(hot_h, column(halo_row), 0, grid_rows, 0)
    for n in range(5, len(pairs)):
        loads[n].start()
    loads[1].wait()
    outgoing[...] = mm(hot_h[...], ext[0:grid_rows, :]).astype(BF16)
    pl.semaphore_wait(barrier, n_group + 1)

    def remote(src, dst, send, recv, where):
        return pltpu.make_async_remote_copy(
            src_ref=src,
            dst_ref=dst,
            send_sem=send,
            recv_sem=recv,
            device_id=where,
            device_id_type=mesh_id,
        )

    up = remote(
        outgoing.at[rim : 2 * rim],
        ext.at[grid_rows : grid_rows + rim],
        halo_send.at[0],
        halo_recv.at[0],
        {"patch": after},
    )
    down = remote(
        outgoing.at[0:rim],
        ext.at[grid_rows + rim : grid_rows + 2 * rim],
        halo_send.at[1],
        halo_recv.at[1],
        {"patch": before},
    )
    up.start()
    down.start()

    slot = lax.broadcasted_iota(jnp.int32, (1, slots), 1)
    own1 = grid_rows + mesh_rows
    for n in (2, 3):
        loads[n].wait()
    sender = e_send_ref[...].reshape(1, slots)
    sender = jnp.where(sender >= grid_rows, sender + mesh_rows, sender)
    target = jnp.where(slot < e_count_ref[0], e_targ_ref[...].reshape(1, slots), -1)
    sender_col, target_col = column(sender), column(target)
    onehot_cols(hot1, sender_col, 0, grid_rows, 0)
    onehot_cols(hot1, target_col, grid_rows, own1, grid_rows)
    onehot_cols(hot1, sender_col, own1, own1 + 2 * rim, 0)
    loads[4].wait()
    tbl1[0:grid_rows, :] = mm(ext[0:grid_rows, :], w_src[...]).astype(BF16)
    loads[5].wait()
    loads[6].wait()
    tbl1[grid_rows:own1, :] = mm(mesh_v[...], w_dst[...]).astype(BF16)

    def chunks(body):
        def step(i, carry):
            body(pl.ds(pl.multiple_of(i * chunk, chunk), chunk))
            return carry

        lax.fori_loop(0, slots // chunk, step, 0)

    def early1(rows):
        acc[rows, :] = mm(hot1[rows, 0:own1], tbl1[0:own1, :])

    chunks(early1)
    onehot_rows(hot1t, sender, 0, grid_rows, 0)
    onehot_rows(hot1t, target, grid_rows, own1, grid_rows)
    onehot_rows(hot1t, sender, own1, own1 + 2 * rim, 0)
    for n in range(7, 11):
        loads[n].wait()
    p_sender = p_send_ref[...].reshape(1, slots)
    local2 = 2 * mesh_rows
    all2 = local2 + coarse.shape[0]
    half = coarse.shape[0] // 2
    row_c = p_sender - mesh_rows
    row_c = ((row_c >> 4) & 1) * half + (row_c >> 5) * COARSE + (row_c & 15)
    p_sender = jnp.where(p_sender >= mesh_rows, row_c + local2, p_sender)
    p_target = jnp.where(slot < p_count_ref[0], p_targ_ref[...].reshape(1, slots), -1)
    p_sender_col, p_target_col = column(p_sender), column(p_target)
    onehot_cols(hot2, p_sender_col, 0, mesh_rows, 0)
    onehot_cols(hot2, p_target_col, mesh_rows, local2, mesh_rows)
    onehot_cols(hot2, p_sender_col, local2, all2, 0)
    onehot_rows(hot2t, p_sender, 0, mesh_rows, 0)
    onehot_rows(hot2t, p_target, mesh_rows, local2, mesh_rows)
    onehot_rows(hot2t, p_sender, local2, all2, 0)
    onehot_rows(hot_ht, halo_row, 0, grid_rows, 0)

    up.wait()
    down.wait()
    tbl1[own1 : own1 + 2 * rim, :] = mm(ext[grid_rows : grid_rows + 2 * rim, :], w_src[...]).astype(
        BF16
    )

    def late1(rows):
        preact = acc[rows, :] + mm(hot1[rows, own1 : own1 + 2 * rim], tbl1[own1 : own1 + 2 * rim, :])
        hid[rows, :] = silu(preact).astype(BF16)
        slope1[rows, :] = preact

    chunks(late1)
    for n in range(11, len(pairs)):
        loads[n].wait()
    summed = mm(hot1t[grid_rows:own1, :], hid[...]).astype(BF16)
    normed1, inverse1 = norm_forward(mm(summed, w_out[...]))
    normed[...] = normed1
    inv[...] = jnp.broadcast_to(inverse1, inv.shape)
    updated = (mesh_v[...].astype(F32) + normed1 * e_gain_ref[...].reshape(1, -1)).astype(BF16)
    projected = mm(updated, p_src[...]).astype(BF16)
    tbl2[0:mesh_rows, :] = projected
    core, level = lax.rem(group, 2), group // 2
    partner = group + 1 - 2 * core
    levels = n_group // 2

    def rows_of(c, z):
        return pl.ds(pl.multiple_of(c * half + z * COARSE, COARSE), COARSE)

    def level_at(k):
        return lax.rem(level + k, levels)

    own_rows = rows_of(core, level)
    far_first = sorted(range(1, levels), key=lambda k: -min(k, levels - k))
    give = remote(
        tbl2.at[0:COARSE], coarse.at[own_rows], co_send.at[0], co_recv.at[0], {"group": partner}
    )
    spread, relay = {}, {}
    for k in far_first:
        spread[k] = remote(
            tbl2.at[0:COARSE],
            coarse.at[own_rows],
            co_send.at[k],
            co_recv.at[k],
            {"group": 2 * level_at(k) + core},
        )
        got = rows_of(core, level_at(levels - k))
        relay[k] = remote(
            coarse.at[got],
            coarse.at[got],
            co_send.at[levels + k],
            co_recv.at[levels + k],
            {"group": partner},
        )
    for k in far_first:
        spread[k].start()
    give.start()
    coarse[own_rows, :] = projected[0:COARSE, :]
    tbl2[mesh_rows:local2, :] = mm(updated, p_dst[...]).astype(BF16)

    def early2(rows):
        acc[rows, :] = mm(hot2[rows, 0:local2], tbl2[...])
        slope1[rows, :] = silu_pair(slope1[rows, :])[1]

    chunks(early2)
    for k in reversed(far_first):
        spread[k].wait_recv()
        relay[k].start()
    give.wait()
    for k in far_first:
        spread[k].wait_send()
    for k in reversed(far_first):
        relay[k].wait()

    def late2(rows):
        preact = acc[rows, :] + mm(hot2[rows, local2:all2], coarse[...])
        hidden, slope = silu_pair(preact)
        hid[rows, :] = hidden.astype(BF16)
        slope2[rows, :] = slope

    chunks(late2)
    summed2 = mm(hot2t[mesh_rows:local2, :], hid[...]).astype(BF16)
    normed2, inverse2 = norm_forward(mm(summed2, p_out[...]))
    cot = cot_v[...].astype(F32)
    node2 = norm_backward(cot * p_gain_ref[...].reshape(1, -1), normed2, inverse2).astype(BF16)
    gnode[...] = mm_t(node2, p_out[...]).astype(BF16)

    def back2(rows):
        grad = mm(hot2[rows, mesh_rows:local2], gnode[...])
        gpre[rows, :] = (grad * slope2[rows, :]).astype(BF16)

    chunks(back2)
    mine = pl.ds(pl.multiple_of(core * half, COARSE), half)
    other = pl.ds(pl.multiple_of((1 - core) * half, COARSE), half)
    swap = remote(gcoarse.at[0], gcoarse.at[1], swap_sem.at[0], swap_sem.at[1], {"group": partner})
    hot2c = hot2t.at[local2:all2]
    gcoarse[0] = mm(hot2c[other, :], gpre[...]).astype(BF16)
    swap.start()
    part = mm(hot2c[mine, :], gpre[...])
    g_local = mm(hot2t[0:mesh_rows, :], gpre[...]).astype(BF16)
    swap.wait()
    gcoarse[2] = (part + gcoarse[1].astype(F32)).astype(BF16)
    scatter = {}
    for k in far_first:
        to = level_at(k)
        scatter[k] = remote(
            gcoarse.at[2, pl.ds(pl.multiple_of(to * COARSE, COARSE), COARSE)],
            rs_buf.at[k - 1],
            rs_send.at[k - 1],
            rs_recv.at[k - 1],
            {"group": 2 * to + core},
        )
    for k in far_first:
        scatter[k].start()
    g_dest = mm(hot2t[mesh_rows:local2, :], gpre[...]).astype(BF16)
    grad_up = cot + mm_t(g_local, p_src[...]) + mm_t(g_dest, p_dst[...])
    gup[...] = grad_up
    gain = e_gain_ref[...].reshape(1, -1)
    node1 = norm_backward(grad_up * gain, normed[...], inv[:, 0:1])
    row = lax.broadcasted_iota(jnp.int32, node1.shape, 0)
    node1 = jnp.where(row < COARSE, 0.0, node1).astype(BF16)
    gnode[...] = mm_t(node1, w_out[...]).astype(BF16)

    def early3(rows):
        acc[rows, :] = mm(hot1[rows, grid_rows:own1], gnode[...])

    chunks(early3)
    gnode16[...] = jnp.zeros_like(gnode16)
    for k in far_first:
        scatter[k].wait()

    total = gcoarse[2, pl.ds(pl.multiple_of(level * COARSE, COARSE), COARSE), :].astype(F32)
    for k in range(levels - 1):
        total = total + rs_buf[k].astype(F32)
    high = total.astype(BF16)
    low = (total - high.astype(F32)).astype(BF16)
    both = mm_t(jnp.concatenate([high, low], axis=0), p_src[...])
    fixed = gup[0:COARSE, :] + both[0:COARSE, :] + both[COARSE:, :]
    gup[0:COARSE, :] = fixed
    node16 = norm_backward(fixed * gain, normed[0:COARSE, :], inv[0:COARSE, 0:1]).astype(BF16)
    gnode16[0:COARSE, :] = mm_t(node16, w_out[...]).astype(BF16)

    def late3(rows):
        grad = acc[rows, :] + mm(hot1[rows, grid_rows : grid_rows + LANES], gnode16[...])
        gpre[rows, :] = (grad * slope1[rows, :]).astype(BF16)

    chunks(late3)
    g_halo[...] = mm(hot1t[own1 : own1 + 2 * rim, :], gpre[...]).astype(BF16)
    back_up = remote(
        g_halo.at[rim : 2 * rim],
        peers.at[0:rim],
        back_send.at[0],
        back_recv.at[0],
        {"patch": after},
    )
    back_down = remote(
        g_halo.at[0:rim],
        peers.at[rim : 2 * rim],
        back_send.at[1],
        back_recv.at[1],
        {"patch": before},
    )
    back_up.start()
    back_down.start()
    g_own = mm(hot1t[0:grid_rows, :], gpre[...]).astype(BF16)
    own[...] = mm_t(g_own, w_src[...])
    g_targ = mm(hot1t[grid_rows:own1, :], gpre[...]).astype(BF16)
    mesh_out[...] = (gup[...] + mm_t(g_targ, w_dst[...])).astype(BF16)
    back_up.wait()
    back_down.wait()
    returned = mm_t(peers[...], w_src[...]).astype(BF16)
    grid_out[...] = (own[...] + mm(hot_ht[...], returned)).astype(BF16)


def on_device(
    n_patch,
    n_group,
    grid_latent,
    mesh_latent,
    cotangent,
    halo_rows,
    encoder_sender,
    encoder_target,
    encoder_count,
    process_sender,
    process_target,
    process_count,
    encoder_source,
    encoder_dest,
    encoder_output,
    encoder_gain,
    process_source,
    process_dest,
    process_output,
    process_gain,
):
    g, d = grid_latent.shape
    m = mesh_latent.shape[0]
    h2 = halo_rows.shape[0]
    e = encoder_sender.shape[0]
    nc = n_group * COARSE
    hbm = pl.BlockSpec(memory_space=pltpu.MemorySpace.HBM)
    smem = pl.BlockSpec(memory_space=pltpu.SMEM)
    vmem = pl.BlockSpec(memory_space=pltpu.VMEM)
    dma = pltpu.SemaphoreType.DMA
    out = pl.pallas_call(
        functools.partial(kernel, n_patch, n_group),
        out_shape=(
            jax.ShapeDtypeStruct((g, d), BF16),
            jax.ShapeDtypeStruct((m, d), BF16),
        ),
        in_specs=[hbm] * 12 + [smem] + [hbm] * 2 + [smem] + [hbm] * 2,
        out_specs=(vmem, vmem),
        scratch_shapes=[
            pltpu.VMEM((g + h2, d), BF16),
            pltpu.VMEM((m, d), BF16),
            pltpu.VMEM((m, d), BF16),
        ]
        + [pltpu.VMEM((d, d), BF16)] * 6
        + [
            pltpu.VMEM((h2, d), BF16),
            pltpu.VMEM((h2, g), BF16),
            pltpu.VMEM((g, h2), BF16),
            pltpu.VMEM((e, g + m + h2), BF16),
            pltpu.VMEM((g + m + h2, e), BF16),
            pltpu.VMEM((e, 2 * m + nc), BF16),
            pltpu.VMEM((2 * m + nc, e), BF16),
            pltpu.VMEM((g + m + h2, d), BF16),
            pltpu.VMEM((2 * m, d), BF16),
            pltpu.VMEM((nc, d), BF16),
            pltpu.VMEM((e, d), F32),
            pltpu.VMEM((e, d), F32),
            pltpu.VMEM((e, d), F32),
            pltpu.VMEM((e, d), BF16),
            pltpu.VMEM((e, d), BF16),
            pltpu.VMEM((m, d), F32),
            pltpu.VMEM((m, LANES), F32),
            pltpu.VMEM((m, d), F32),
            pltpu.VMEM((m, d), BF16),
            pltpu.VMEM((LANES, d), BF16),
            pltpu.VMEM((3, nc // 2, d), BF16),
            pltpu.VMEM((n_group // 2 - 1, COARSE, d), BF16),
            pltpu.VMEM((h2, d), BF16),
            pltpu.VMEM((h2, d), BF16),
            pltpu.VMEM((g, d), F32),
            pltpu.VMEM((h2,), jnp.int32),
            pltpu.VMEM((e,), jnp.int32),
            pltpu.VMEM((e,), jnp.int32),
            pltpu.VMEM((e,), jnp.int32),
            pltpu.VMEM((e,), jnp.int32),
            pltpu.VMEM((d,), F32),
            pltpu.VMEM((d,), F32),
            dma((16,)),
            dma((2,)),
            dma((2,)),
            dma((n_group,)),
            dma((n_group,)),
            dma((2,)),
            dma((n_group // 2 - 1,)),
            dma((n_group // 2 - 1,)),
            dma((2,)),
            dma((2,)),
        ],
        compiler_params=pltpu.CompilerParams(
            collective_id=0, has_side_effects=True, vmem_limit_bytes=40 * 1024 * 1024
        ),
        name="step",
    )(
        *[
            x if x.size == 1 else pltpu.with_memory_space_constraint(x, pltpu.MemorySpace.HBM)
            for x in (
        grid_latent,
        mesh_latent,
        cotangent,
        encoder_source,
        encoder_dest,
        encoder_output,
        process_source,
        process_dest,
        process_output,
        halo_rows,
        encoder_sender,
        encoder_target,
        encoder_count,
        process_sender,
        process_target,
        process_count,
        encoder_gain,
        process_gain,
            )
        ]
    )
    return out


def solution(mesh):
    both = P(("patch", "group"))
    rows = P(("patch", "group"), None)
    return jax.shard_map(
        functools.partial(on_device, mesh.shape["patch"], mesh.shape["group"]),
        mesh=mesh,
        in_specs=(rows,) * 3 + (both,) * 7 + (P(),) * 8,
        out_specs=(rows, rows),
        check_vma=False,
    )
```

```python
import functools

import jax
import jax.numpy as jnp
from jax import lax
from jax.experimental import pallas as pl
from jax.experimental.pallas import tpu as pltpu
from jax.sharding import PartitionSpec as P

EPSILON = 1e-05
F32 = jnp.float32
BF16 = jnp.bfloat16
COARSE = 16
LANES = 128


def mm(a, b):
    return jnp.dot(a, b, preferred_element_type=F32)


def mm_t(a, b):
    return lax.dot_general(a, b, (((1,), (1,)), ((), ())), preferred_element_type=F32)


def column(row):
    return jnp.transpose(jnp.broadcast_to(row, (LANES, row.shape[1])))


def onehot_cols(ref, col, start, stop, shift):
    lane = lax.broadcasted_iota(jnp.int32, (col.shape[0], LANES), 1)
    for c in range(start, stop, LANES):
        width = min(LANES, stop - c)
        hit = jnp.where(col == lane + (c - shift), 1.0, 0.0).astype(BF16)
        ref[:, c : c + width] = hit[:, :width]


def onehot_rows(ref, row, start, stop, shift):
    for c in range(start, stop, LANES):
        height = min(LANES, stop - c)
        sub = lax.broadcasted_iota(jnp.int32, (height, row.shape[1]), 0)
        hit = jnp.where(row == sub + (c - shift), 1.0, 0.0).astype(BF16)
        ref[c : c + height, :] = hit


def norm_backward(scaled, normed, inverse):
    first = jnp.mean(scaled, axis=-1, keepdims=True)
    second = jnp.mean(scaled * normed, axis=-1, keepdims=True)
    return inverse * (scaled - first - normed * second)


def norm_forward(values):
    center = values - jnp.mean(values, axis=-1, keepdims=True)
    inverse = lax.rsqrt(jnp.mean(center * center, axis=-1, keepdims=True) + EPSILON)
    return center * inverse, inverse


def silu_pair(values):
    logistic = 0.5 * jnp.tanh(0.5 * values) + 0.5
    hidden = values * logistic
    return hidden, logistic + hidden * (1.0 - logistic)


def silu(values):
    return values * (0.5 * jnp.tanh(0.5 * values) + 0.5)


def kernel(
    n_patch,
    n_group,
    grid_hbm,
    mesh_hbm,
    cot_hbm,
    w_src_hbm,
    w_dst_hbm,
    w_out_hbm,
    p_src_hbm,
    p_dst_hbm,
    p_out_hbm,
    halo_ref,
    e_send_hbm,
    e_targ_hbm,
    e_count_ref,
    p_send_hbm,
    p_targ_hbm,
    p_count_ref,
    e_gain_hbm,
    p_gain_hbm,
    grid_out,
    mesh_out,
    grid_v,
    ext,
    mesh_v,
    cot_v,
    w_src,
    w_dst,
    w_out,
    p_src,
    p_dst,
    p_out,
    outgoing,
    hot_h,
    hot_ht,
    hot1,
    hot1t,
    hot2,
    hot2t,
    tbl1,
    tbl2,
    coarse,
    coarse16,
    acc,
    slope1,
    slope2,
    hid,
    gpre,
    normed,
    inv,
    gup,
    gnode,
    gnode16,
    gcoarse,
    joint,
    rs_buf,
    g_halo,
    peers,
    own,
    e_send_ref,
    e_targ_ref,
    p_send_ref,
    p_targ_ref,
    e_gain_ref,
    p_gain_ref,
    grid_sem,
    load_sem,
    halo_send,
    halo_recv,
    co_send,
    co_recv,
    swap_sem,
    rs_send,
    rs_recv,
    back_send,
    back_recv,
):
    patch, group = lax.axis_index("patch"), lax.axis_index("group")
    after = lax.rem(patch + 1, n_patch)
    before = lax.rem(patch + n_patch - 1, n_patch)
    grid_rows, mesh_rows = grid_v.shape[0], mesh_hbm.shape[0]
    rim = outgoing.shape[0] // 2
    slots = e_send_ref.shape[0]
    chunk = 256
    mesh_id = pl.DeviceIdType.MESH

    pairs = (
        (e_send_hbm, e_send_ref),
        (e_targ_hbm, e_targ_ref),
        (w_src_hbm, w_src),
        (mesh_hbm, mesh_v),
        (w_dst_hbm, w_dst),
        (p_send_hbm, p_send_ref),
        (p_targ_hbm, p_targ_ref),
        (e_gain_hbm, e_gain_ref),
        (p_gain_hbm, p_gain_ref),
        (w_out_hbm, w_out),
        (p_src_hbm, p_src),
        (p_dst_hbm, p_dst),
        (p_out_hbm, p_out),
        (cot_hbm, cot_v),
    )
    loads = [
        pltpu.make_async_copy(src, dst, load_sem.at[n]) for n, (src, dst) in enumerate(pairs)
    ]
    quarter = grid_rows // 4
    first = [
        pltpu.make_async_copy(
            grid_hbm.at[n * quarter : (n + 1) * quarter],
            grid_v.at[n * quarter : (n + 1) * quarter],
            grid_sem.at[n],
        )
        for n in range(4)
    ]
    for copy in first:
        copy.start()
    barrier = pltpu.get_barrier_semaphore()
    for neighbour in (before, after):
        pl.semaphore_signal(
            barrier, inc=1, device_id={"patch": neighbour}, device_id_type=mesh_id
        )

    core, level = lax.rem(group, 2), group // 2
    levels = n_group // 2
    partner = group + 1 - 2 * core

    def level_at(k):
        return lax.rem(level + k, levels)

    contacts = [partner] + [2 * level_at(k) + core for k in range(1, levels)]
    for peer in contacts:
        pl.semaphore_signal(barrier, inc=1, device_id={"group": peer}, device_id_type=mesh_id)

    halo_row = halo_ref[...].reshape(1, 2 * rim)
    onehot_cols(hot_h, column(halo_row), 0, grid_rows, 0)
    for copy in first:
        copy.wait()
    outgoing[...] = mm(hot_h[...], grid_v[...]).astype(BF16)
    pl.semaphore_wait(barrier, 2 + len(contacts))

    def remote(src, dst, send, recv, where):
        return pltpu.make_async_remote_copy(
            src_ref=src,
            dst_ref=dst,
            send_sem=send,
            recv_sem=recv,
            device_id=where,
            device_id_type=mesh_id,
        )

    up = remote(
        outgoing.at[rim : 2 * rim],
        ext.at[0:rim],
        halo_send.at[0],
        halo_recv.at[0],
        {"patch": after},
    )
    down = remote(
        outgoing.at[0:rim],
        ext.at[rim : 2 * rim],
        halo_send.at[1],
        halo_recv.at[1],
        {"patch": before},
    )
    up.start()
    down.start()
    for copy in loads:
        copy.start()

    slot = lax.broadcasted_iota(jnp.int32, (1, slots), 1)
    own1 = grid_rows + mesh_rows
    for n in (0, 1):
        loads[n].wait()
    sender = e_send_ref[...].reshape(1, slots)
    sender = jnp.where(sender >= grid_rows, sender + mesh_rows, sender)
    target = jnp.where(slot < e_count_ref[0], e_targ_ref[...].reshape(1, slots), -1)
    sender_col, target_col = column(sender), column(target)
    onehot_cols(hot1, sender_col, 0, grid_rows, 0)
    onehot_cols(hot1, target_col, grid_rows, own1, grid_rows)
    onehot_cols(hot1, sender_col, own1, own1 + 2 * rim, 0)
    loads[2].wait()
    tbl1[0:grid_rows, :] = mm(grid_v[...], w_src[...]).astype(BF16)
    loads[3].wait()
    loads[4].wait()
    tbl1[grid_rows:own1, :] = mm(mesh_v[...], w_dst[...]).astype(BF16)

    def chunks(body):
        for i in range(0, slots, chunk):
            body(slice(i, i + chunk))

    def early1(rows):
        acc[rows, :] = mm(hot1[rows, 0:own1], tbl1[0:own1, :])

    chunks(early1)
    onehot_rows(hot1t, sender, 0, grid_rows, 0)
    onehot_rows(hot1t, target, grid_rows, own1, grid_rows)
    onehot_rows(hot1t, sender, own1, own1 + 2 * rim, 0)
    for n in range(5, 9):
        loads[n].wait()
    p_sender = p_send_ref[...].reshape(1, slots)
    local2 = 2 * mesh_rows
    all2 = local2 + coarse.shape[0]
    half = coarse.shape[0] // 2
    row_c = p_sender - mesh_rows
    row_c = ((row_c >> 4) & 1) * half + (row_c >> 5) * COARSE + (row_c & 15)
    p_sender = jnp.where(p_sender >= mesh_rows, row_c + local2, p_sender)
    p_target = jnp.where(slot < p_count_ref[0], p_targ_ref[...].reshape(1, slots), -1)
    p_sender_col, p_target_col = column(p_sender), column(p_target)
    onehot_cols(hot2, p_sender_col, 0, mesh_rows, 0)
    onehot_cols(hot2, p_target_col, mesh_rows, local2, mesh_rows)
    onehot_cols(hot2, p_sender_col, local2, all2, 0)
    onehot_rows(hot2t, p_sender, 0, mesh_rows, 0)
    onehot_rows(hot2t, p_target, mesh_rows, local2, mesh_rows)
    onehot_rows(hot2t, p_sender, local2, all2, 0)
    onehot_rows(hot_ht, halo_row, 0, grid_rows, 0)

    up.wait()
    down.wait()
    tbl1[own1 : own1 + 2 * rim, :] = mm(ext[...], w_src[...]).astype(BF16)

    def late1(rows):
        preact = acc[rows, :] + mm(hot1[rows, own1 : own1 + 2 * rim], tbl1[own1 : own1 + 2 * rim, :])
        hid[rows, :] = silu(preact).astype(BF16)
        slope1[rows, :] = preact

    chunks(late1)
    for n in range(9, len(pairs)):
        loads[n].wait()
    summed16 = mm(hot1t[grid_rows : grid_rows + COARSE, :], hid[...]).astype(BF16)
    normed16 = norm_forward(mm(summed16, w_out[...]))[0]
    mesh16 = mesh_v[0:COARSE, :].astype(F32)
    updated16 = (mesh16 + normed16 * e_gain_ref[...].reshape(1, -1)).astype(BF16)
    coarse16[...] = mm(updated16, p_src[...]).astype(BF16)

    def rows_of(c, z):
        return pl.ds(pl.multiple_of(c * half + z * COARSE, COARSE), COARSE)

    own_rows = rows_of(core, level)
    far_first = sorted(range(1, levels), key=lambda k: -min(k, levels - k))
    give = remote(
        coarse16, coarse.at[own_rows], co_send.at[0], co_recv.at[0], {"group": partner}
    )
    spread, relay = {}, {}
    for k in far_first:
        spread[k] = remote(
            coarse16,
            coarse.at[own_rows],
            co_send.at[k],
            co_recv.at[k],
            {"group": 2 * level_at(k) + core},
        )
        got = rows_of(core, level_at(levels - k))
        relay[k] = remote(
            coarse.at[got],
            coarse.at[got],
            co_send.at[levels + k],
            co_recv.at[levels + k],
            {"group": partner},
        )
    for k in far_first:
        spread[k].start()
    give.start()
    coarse[own_rows, :] = coarse16[...]
    summed = mm(hot1t[grid_rows:own1, :], hid[...]).astype(BF16)
    normed1, inverse1 = norm_forward(mm(summed, w_out[...]))
    normed[...] = normed1
    inv[...] = jnp.broadcast_to(inverse1, inv.shape)
    updated = (mesh_v[...].astype(F32) + normed1 * e_gain_ref[...].reshape(1, -1)).astype(BF16)
    projected = mm(updated, p_src[...]).astype(BF16)
    tbl2[0:mesh_rows, :] = projected
    tbl2[mesh_rows:local2, :] = mm(updated, p_dst[...]).astype(BF16)

    def early2(rows):
        acc[rows, :] = mm(hot2[rows, 0:local2], tbl2[...])
        slope1[rows, :] = silu_pair(slope1[rows, :])[1]

    chunks(early2)
    for k in reversed(far_first):
        spread[k].wait_recv()
        relay[k].start()
    give.wait()
    for k in far_first:
        spread[k].wait_send()
    for k in reversed(far_first):
        relay[k].wait()

    def late2(rows):
        preact = acc[rows, :] + mm(hot2[rows, local2:all2], coarse[...])
        hidden, slope = silu_pair(preact)
        hid[rows, :] = hidden.astype(BF16)
        slope2[rows, :] = slope

    chunks(late2)
    summed2 = mm(hot2t[mesh_rows:local2, :], hid[...]).astype(BF16)
    normed2, inverse2 = norm_forward(mm(summed2, p_out[...]))
    cot = cot_v[...].astype(F32)
    node2 = norm_backward(cot * p_gain_ref[...].reshape(1, -1), normed2, inverse2).astype(BF16)
    gnode[...] = mm_t(node2, p_out[...]).astype(BF16)

    def back2(rows):
        grad = mm(hot2[rows, mesh_rows:local2], gnode[...])
        gpre[rows, :] = (grad * slope2[rows, :]).astype(BF16)

    chunks(back2)
    mine = pl.ds(pl.multiple_of(core * half, COARSE), half)
    other = pl.ds(pl.multiple_of((1 - core) * half, COARSE), half)
    swap = remote(gcoarse.at[0], gcoarse.at[1], swap_sem.at[0], swap_sem.at[1], {"group": partner})
    hot2c = hot2t.at[local2:all2]
    gcoarse[0] = mm(hot2c[other, :], gpre[...]).astype(BF16)
    swap.start()
    gcoarse[2] = mm(hot2c[mine, :], gpre[...]).astype(BF16)
    g_local = mm(hot2t[0:mesh_rows, :], gpre[...]).astype(BF16)
    swap.wait()
    scatter = {}
    for k in far_first + [0]:
        to = level_at(k)
        rows = pl.ds(pl.multiple_of(to * COARSE, COARSE), COARSE)
        joint[k] = (gcoarse[2, rows, :].astype(F32) + gcoarse[1, rows, :].astype(F32)).astype(BF16)
        if k:
            scatter[k] = remote(
                joint.at[k],
                rs_buf.at[k - 1],
                rs_send.at[k - 1],
                rs_recv.at[k - 1],
                {"group": 2 * to + core},
            )
            scatter[k].start()
    g_dest = mm(hot2t[mesh_rows:local2, :], gpre[...]).astype(BF16)
    grad_up = cot + mm_t(g_local, p_src[...]) + mm_t(g_dest, p_dst[...])
    gup[...] = grad_up
    gain = e_gain_ref[...].reshape(1, -1)
    node1 = norm_backward(grad_up * gain, normed[...], inv[:, 0:1])
    row = lax.broadcasted_iota(jnp.int32, node1.shape, 0)
    node1 = jnp.where(row < COARSE, 0.0, node1).astype(BF16)
    gnode[...] = mm_t(node1, w_out[...]).astype(BF16)

    def early3(rows):
        acc[rows, :] = mm(hot1[rows, grid_rows:own1], gnode[...])

    chunks(early3)
    gnode16[...] = jnp.zeros_like(gnode16)
    for k in far_first:
        scatter[k].wait()

    total = joint[0].astype(F32)
    for k in range(levels - 1):
        total = total + rs_buf[k].astype(F32)
    high = total.astype(BF16)
    low = (total - high.astype(F32)).astype(BF16)
    both = mm_t(jnp.concatenate([high, low], axis=0), p_src[...])
    fixed = gup[0:COARSE, :] + both[0:COARSE, :] + both[COARSE:, :]
    gup[0:COARSE, :] = fixed
    node16 = norm_backward(fixed * gain, normed[0:COARSE, :], inv[0:COARSE, 0:1]).astype(BF16)
    gnode16[0:COARSE, :] = mm_t(node16, w_out[...]).astype(BF16)

    def late3(rows):
        grad = acc[rows, :] + mm(hot1[rows, grid_rows : grid_rows + LANES], gnode16[...])
        gpre[rows, :] = (grad * slope1[rows, :]).astype(BF16)

    chunks(late3)
    g_halo[...] = mm(hot1t[own1 : own1 + 2 * rim, :], gpre[...]).astype(BF16)
    back_up = remote(
        g_halo.at[rim : 2 * rim],
        peers.at[0:rim],
        back_send.at[0],
        back_recv.at[0],
        {"patch": after},
    )
    back_down = remote(
        g_halo.at[0:rim],
        peers.at[rim : 2 * rim],
        back_send.at[1],
        back_recv.at[1],
        {"patch": before},
    )
    back_up.start()
    back_down.start()
    g_own = mm(hot1t[0:grid_rows, :], gpre[...]).astype(BF16)
    own[...] = mm_t(g_own, w_src[...])
    g_targ = mm(hot1t[grid_rows:own1, :], gpre[...]).astype(BF16)
    mesh_out[...] = (gup[...] + mm_t(g_targ, w_dst[...])).astype(BF16)
    back_down.wait()
    returned = mm_t(peers[rim : 2 * rim, :], w_src[...]).astype(BF16)
    own[...] += mm(hot_ht[:, rim : 2 * rim], returned)
    back_up.wait()
    returned = mm_t(peers[0:rim, :], w_src[...]).astype(BF16)
    grid_out[...] = (own[...] + mm(hot_ht[:, 0:rim], returned)).astype(BF16)


def write_out(grid_ref, mesh_ref, grid_out, mesh_out, sem):
    copies = [
        pltpu.make_async_copy(grid_ref, grid_out, sem.at[0]),
        pltpu.make_async_copy(mesh_ref, mesh_out, sem.at[1]),
    ]
    for copy in copies:
        copy.start()
    for copy in copies:
        copy.wait()


def on_device(
    n_patch,
    n_group,
    grid_latent,
    mesh_latent,
    cotangent,
    halo_rows,
    encoder_sender,
    encoder_target,
    encoder_count,
    process_sender,
    process_target,
    process_count,
    encoder_source,
    encoder_dest,
    encoder_output,
    encoder_gain,
    process_source,
    process_dest,
    process_output,
    process_gain,
):
    g, d = grid_latent.shape
    m = mesh_latent.shape[0]
    h2 = halo_rows.shape[0]
    e = encoder_sender.shape[0]
    nc = n_group * COARSE
    hbm = pl.BlockSpec(memory_space=pltpu.MemorySpace.HBM)
    smem = pl.BlockSpec(memory_space=pltpu.SMEM)
    vmem = pl.BlockSpec(memory_space=pltpu.VMEM)
    dma = pltpu.SemaphoreType.DMA
    out = pl.pallas_call(
        functools.partial(kernel, n_patch, n_group),
        out_shape=(
            jax.ShapeDtypeStruct((g, d), BF16),
            jax.ShapeDtypeStruct((m, d), BF16),
        ),
        in_specs=[hbm] * 9 + [vmem] + [hbm] * 2 + [smem] + [hbm] * 2 + [smem] + [hbm] * 2,
        out_specs=(vmem, vmem),
        scratch_shapes=[
            pltpu.VMEM((g, d), BF16),
            pltpu.VMEM((h2, d), BF16),
            pltpu.VMEM((m, d), BF16),
            pltpu.VMEM((m, d), BF16),
        ]
        + [pltpu.VMEM((d, d), BF16)] * 6
        + [
            pltpu.VMEM((h2, d), BF16),
            pltpu.VMEM((h2, g), BF16),
            pltpu.VMEM((g, h2), BF16),
            pltpu.VMEM((e, g + m + h2), BF16),
            pltpu.VMEM((g + m + h2, e), BF16),
            pltpu.VMEM((e, 2 * m + nc), BF16),
            pltpu.VMEM((2 * m + nc, e), BF16),
            pltpu.VMEM((g + m + h2, d), BF16),
            pltpu.VMEM((2 * m, d), BF16),
            pltpu.VMEM((nc, d), BF16),
            pltpu.VMEM((COARSE, d), BF16),
            pltpu.VMEM((e, d), F32),
            pltpu.VMEM((e, d), F32),
            pltpu.VMEM((e, d), F32),
            pltpu.VMEM((e, d), BF16),
            pltpu.VMEM((e, d), BF16),
            pltpu.VMEM((m, d), F32),
            pltpu.VMEM((m, LANES), F32),
            pltpu.VMEM((m, d), F32),
            pltpu.VMEM((m, d), BF16),
            pltpu.VMEM((LANES, d), BF16),
            pltpu.VMEM((3, nc // 2, d), BF16),
            pltpu.VMEM((n_group // 2, COARSE, d), BF16),
            pltpu.VMEM((n_group // 2 - 1, COARSE, d), BF16),
            pltpu.VMEM((h2, d), BF16),
            pltpu.VMEM((h2, d), BF16),
            pltpu.VMEM((g, d), F32),
            pltpu.VMEM((e,), jnp.int32),
            pltpu.VMEM((e,), jnp.int32),
            pltpu.VMEM((e,), jnp.int32),
            pltpu.VMEM((e,), jnp.int32),
            pltpu.VMEM((d,), F32),
            pltpu.VMEM((d,), F32),
            dma((4,)),
            dma((14,)),
            dma((2,)),
            dma((2,)),
            dma((n_group,)),
            dma((n_group,)),
            dma((2,)),
            dma((n_group // 2 - 1,)),
            dma((n_group // 2 - 1,)),
            dma((2,)),
            dma((2,)),
        ],
        compiler_params=pltpu.CompilerParams(
            collective_id=0, has_side_effects=True, vmem_limit_bytes=40 * 1024 * 1024
        ),
        name="step",
    )(
        *[
            x if n in (9, 12, 15) else pltpu.with_memory_space_constraint(x, pltpu.MemorySpace.HBM)
            for n, x in enumerate((
        grid_latent,
        mesh_latent,
        cotangent,
        encoder_source,
        encoder_dest,
        encoder_output,
        process_source,
        process_dest,
        process_output,
        halo_rows,
        encoder_sender,
        encoder_target,
        encoder_count,
        process_sender,
        process_target,
        process_count,
        encoder_gain,
        process_gain,
            ))
        ]
    )
    out = [pltpu.with_memory_space_constraint(x, pltpu.MemorySpace.VMEM) for x in out]
    return pl.pallas_call(
        write_out,
        out_shape=(jax.ShapeDtypeStruct((g, d), BF16), jax.ShapeDtypeStruct((m, d), BF16)),
        in_specs=[vmem, vmem],
        out_specs=(hbm, hbm),
        scratch_shapes=[dma((2,))],
        name="write_out",
    )(*out)


def solution(mesh):
    both = P(("patch", "group"))
    rows = P(("patch", "group"), None)
    return jax.shard_map(
        functools.partial(on_device, mesh.shape["patch"], mesh.shape["group"]),
        mesh=mesh,
        in_specs=(rows,) * 3 + (both,) * 7 + (P(),) * 8,
        out_specs=(rows, rows),
        check_vma=False,
    )
```

```python
import functools

import jax
import jax.numpy as jnp
from jax import lax
from jax.experimental import pallas as pl
from jax.experimental.pallas import tpu as pltpu
from jax.sharding import PartitionSpec as P

EPSILON = 1e-05
F32 = jnp.float32
BF16 = jnp.bfloat16
COARSE = 16
LANES = 128


def mm(a, b):
    return jnp.dot(a, b, preferred_element_type=F32)


def mm_t(a, b):
    return lax.dot_general(a, b, (((1,), (1,)), ((), ())), preferred_element_type=F32)


def column(row):
    return jnp.transpose(jnp.broadcast_to(row, (LANES, row.shape[1])))


def onehot_cols(ref, col, start, stop, shift):
    lane = lax.broadcasted_iota(jnp.int32, (col.shape[0], LANES), 1)
    for c in range(start, stop, LANES):
        width = min(LANES, stop - c)
        hit = jnp.where(col == lane + (c - shift), 1.0, 0.0).astype(BF16)
        ref[:, c : c + width] = hit[:, :width]


def onehot_rows(ref, row, start, stop, shift):
    for c in range(start, stop, LANES):
        height = min(LANES, stop - c)
        sub = lax.broadcasted_iota(jnp.int32, (height, row.shape[1]), 0)
        hit = jnp.where(row == sub + (c - shift), 1.0, 0.0).astype(BF16)
        ref[c : c + height, :] = hit


def norm_backward(scaled, normed, inverse):
    first = jnp.mean(scaled, axis=-1, keepdims=True)
    second = jnp.mean(scaled * normed, axis=-1, keepdims=True)
    return inverse * (scaled - first - normed * second)


def norm_forward(values):
    center = values - jnp.mean(values, axis=-1, keepdims=True)
    inverse = lax.rsqrt(jnp.mean(center * center, axis=-1, keepdims=True) + EPSILON)
    return center * inverse, inverse


def silu_pair(values):
    logistic = 0.5 * jnp.tanh(0.5 * values) + 0.5
    hidden = values * logistic
    return hidden, logistic + hidden * (1.0 - logistic)


def silu(values):
    return values * (0.5 * jnp.tanh(0.5 * values) + 0.5)


def kernel(
    n_patch,
    n_group,
    grid_hbm,
    mesh_hbm,
    cot_hbm,
    w_src_hbm,
    w_dst_hbm,
    w_out_hbm,
    p_src_hbm,
    p_dst_hbm,
    p_out_hbm,
    halo_ref,
    e_send_hbm,
    e_targ_hbm,
    e_count_ref,
    p_send_hbm,
    p_targ_hbm,
    p_count_ref,
    e_gain_hbm,
    p_gain_hbm,
    grid_out,
    mesh_out,
    grid_v,
    ext,
    mesh_v,
    cot_v,
    w_src,
    w_dst,
    w_out,
    p_src,
    p_dst,
    p_out,
    outgoing,
    hot_h,
    hot_ht,
    hot1,
    hot1t,
    hot2,
    hot2t,
    tbl1,
    tbl2,
    coarse,
    coarse16,
    acc,
    slope1,
    slope2,
    hid,
    gpre,
    normed,
    inv,
    gup,
    gnode,
    gnode16,
    gcoarse,
    joint,
    rs_buf,
    g_halo,
    peers,
    own,
    e_send_ref,
    e_targ_ref,
    p_send_ref,
    p_targ_ref,
    e_gain_ref,
    p_gain_ref,
    grid_sem,
    load_sem,
    halo_send,
    halo_recv,
    co_send,
    co_recv,
    swap_sem,
    rs_send,
    rs_recv,
    back_send,
    back_recv,
):
    patch, group = lax.axis_index("patch"), lax.axis_index("group")
    after = lax.rem(patch + 1, n_patch)
    before = lax.rem(patch + n_patch - 1, n_patch)
    grid_rows, mesh_rows = grid_v.shape[0], mesh_hbm.shape[0]
    rim = outgoing.shape[0] // 2
    slots = e_send_ref.shape[0]
    chunk = 384
    mesh_id = pl.DeviceIdType.MESH

    core, level = lax.rem(group, 2), group // 2
    levels = n_group // 2
    partner = group + 1 - 2 * core

    def level_at(k):
        return lax.rem(level + k, levels)

    far_first = sorted(range(1, levels), key=lambda k: -min(k, levels - k))
    contacts = [{"group": 2 * level_at(k) + core} for k in far_first]
    contacts += [{"patch": before}, {"patch": after}, {"group": partner}]
    barrier = pltpu.get_barrier_semaphore()
    for where in contacts:
        pl.semaphore_signal(barrier, inc=1, device_id=where, device_id_type=mesh_id)

    pairs = (
        (e_send_hbm, e_send_ref),
        (e_targ_hbm, e_targ_ref),
        (w_src_hbm, w_src),
        (mesh_hbm, mesh_v),
        (w_dst_hbm, w_dst),
        (p_send_hbm, p_send_ref),
        (p_targ_hbm, p_targ_ref),
        (e_gain_hbm, e_gain_ref),
        (p_gain_hbm, p_gain_ref),
        (w_out_hbm, w_out),
        (p_src_hbm, p_src),
        (p_dst_hbm, p_dst),
        (p_out_hbm, p_out),
        (cot_hbm, cot_v),
    )
    loads = [
        pltpu.make_async_copy(src, dst, load_sem.at[n]) for n, (src, dst) in enumerate(pairs)
    ]
    quarter = grid_rows // 4
    first = [
        pltpu.make_async_copy(
            grid_hbm.at[n * quarter : (n + 1) * quarter],
            grid_v.at[n * quarter : (n + 1) * quarter],
            grid_sem.at[n],
        )
        for n in range(4)
    ]
    for copy in first + [loads[2]]:
        copy.start()

    halo_row = halo_ref[...].reshape(1, 2 * rim)
    onehot_cols(hot_h, column(halo_row), 0, grid_rows, 0)
    for copy in first + [loads[2]]:
        copy.wait()
    tbl1[0:grid_rows, :] = mm(grid_v[...], w_src[...]).astype(BF16)
    outgoing[...] = mm(hot_h[...], tbl1[0:grid_rows, :]).astype(BF16)
    pl.semaphore_wait(barrier, len(contacts))

    def remote(src, dst, send, recv, where):
        return pltpu.make_async_remote_copy(
            src_ref=src,
            dst_ref=dst,
            send_sem=send,
            recv_sem=recv,
            device_id=where,
            device_id_type=mesh_id,
        )

    up = remote(
        outgoing.at[rim : 2 * rim],
        ext.at[0:rim],
        halo_send.at[0],
        halo_recv.at[0],
        {"patch": after},
    )
    down = remote(
        outgoing.at[0:rim],
        ext.at[rim : 2 * rim],
        halo_send.at[1],
        halo_recv.at[1],
        {"patch": before},
    )
    up.start()
    down.start()
    for copy in loads[:2] + loads[3:]:
        copy.start()

    slot = lax.broadcasted_iota(jnp.int32, (1, slots), 1)
    own1 = grid_rows + mesh_rows
    for n in (0, 1):
        loads[n].wait()
    sender = e_send_ref[...].reshape(1, slots)
    sender = jnp.where(sender >= grid_rows, sender + mesh_rows, sender)
    target = jnp.where(slot < e_count_ref[0], e_targ_ref[...].reshape(1, slots), -1)
    sender_col, target_col = column(sender), column(target)
    onehot_cols(hot1, sender_col, 0, grid_rows, 0)
    onehot_cols(hot1, target_col, grid_rows, own1, grid_rows)
    onehot_cols(hot1, sender_col, own1, own1 + 2 * rim, 0)
    loads[3].wait()
    loads[4].wait()
    tbl1[grid_rows:own1, :] = mm(mesh_v[...], w_dst[...]).astype(BF16)

    def chunks(body):
        for i in range(0, slots, chunk):
            body(slice(i, i + chunk))

    def early1(rows):
        acc[rows, :] = mm(hot1[rows, 0:own1], tbl1[0:own1, :])

    chunks(early1)
    onehot_rows(hot1t, sender, 0, grid_rows, 0)
    onehot_rows(hot1t, target, grid_rows, own1, grid_rows)
    onehot_rows(hot1t, sender, own1, own1 + 2 * rim, 0)
    for n in range(5, 9):
        loads[n].wait()
    p_sender = p_send_ref[...].reshape(1, slots)
    local2 = 2 * mesh_rows
    all2 = local2 + coarse.shape[0]
    half = coarse.shape[0] // 2
    row_c = p_sender - mesh_rows
    row_c = ((row_c >> 4) & 1) * half + (row_c >> 5) * COARSE + (row_c & 15)
    p_sender = jnp.where(p_sender >= mesh_rows, row_c + local2, p_sender)
    p_target = jnp.where(slot < p_count_ref[0], p_targ_ref[...].reshape(1, slots), -1)
    p_sender_col, p_target_col = column(p_sender), column(p_target)
    onehot_cols(hot2, p_sender_col, 0, mesh_rows, 0)
    onehot_cols(hot2, p_target_col, mesh_rows, local2, mesh_rows)
    onehot_cols(hot2, p_sender_col, local2, all2, 0)
    onehot_rows(hot2t, p_sender, 0, mesh_rows, 0)
    onehot_rows(hot2t, p_target, mesh_rows, local2, mesh_rows)
    onehot_rows(hot2t, p_sender, local2, all2, 0)
    onehot_rows(hot_ht, halo_row, 0, grid_rows, 0)

    up.wait()
    down.wait()
    def late1(rows):
        preact = acc[rows, :] + mm(hot1[rows, own1 : own1 + 2 * rim], ext[...])
        hid[rows, :] = silu(preact).astype(BF16)
        slope1[rows, :] = preact

    chunks(late1)
    for n in range(9, len(pairs)):
        loads[n].wait()
    summed16 = mm(hot1t[grid_rows : grid_rows + COARSE, :], hid[...]).astype(BF16)
    normed16 = norm_forward(mm(summed16, w_out[...]))[0]
    mesh16 = mesh_v[0:COARSE, :].astype(F32)
    updated16 = (mesh16 + normed16 * e_gain_ref[...].reshape(1, -1)).astype(BF16)
    coarse16[...] = mm(updated16, p_src[...]).astype(BF16)

    def rows_of(c, z):
        return pl.ds(pl.multiple_of(c * half + z * COARSE, COARSE), COARSE)

    own_rows = rows_of(core, level)
    give = remote(
        coarse16, coarse.at[own_rows], co_send.at[0], co_recv.at[0], {"group": partner}
    )
    spread, relay = {}, {}
    for k in far_first:
        spread[k] = remote(
            coarse16,
            coarse.at[own_rows],
            co_send.at[k],
            co_recv.at[k],
            {"group": 2 * level_at(k) + core},
        )
        got = rows_of(core, level_at(levels - k))
        relay[k] = remote(
            coarse.at[got],
            coarse.at[got],
            co_send.at[levels + k],
            co_recv.at[levels + k],
            {"group": partner},
        )
    for k in far_first:
        spread[k].start()
    give.start()
    coarse[own_rows, :] = coarse16[...]
    summed = mm(hot1t[grid_rows:own1, :], hid[...]).astype(BF16)
    normed1, inverse1 = norm_forward(mm(summed, w_out[...]))
    normed[...] = normed1
    inv[...] = jnp.broadcast_to(inverse1, inv.shape)
    updated = (mesh_v[...].astype(F32) + normed1 * e_gain_ref[...].reshape(1, -1)).astype(BF16)
    projected = mm(updated, p_src[...]).astype(BF16)
    tbl2[0:mesh_rows, :] = projected
    tbl2[mesh_rows:local2, :] = mm(updated, p_dst[...]).astype(BF16)

    def early2(rows):
        acc[rows, :] = mm(hot2[rows, 0:local2], tbl2[...])
        slope1[rows, :] = silu_pair(slope1[rows, :])[1]

    chunks(early2)
    for k in reversed(far_first):
        spread[k].wait_recv()
        relay[k].start()
    give.wait()
    for k in far_first:
        spread[k].wait_send()
    for k in reversed(far_first):
        relay[k].wait()

    def late2(rows):
        preact = acc[rows, :] + mm(hot2[rows, local2:all2], coarse[...])
        hidden, slope = silu_pair(preact)
        hid[rows, :] = hidden.astype(BF16)
        slope2[rows, :] = slope

    chunks(late2)
    summed2 = mm(hot2t[mesh_rows:local2, :], hid[...]).astype(BF16)
    normed2, inverse2 = norm_forward(mm(summed2, p_out[...]))
    cot = cot_v[...].astype(F32)
    node2 = norm_backward(cot * p_gain_ref[...].reshape(1, -1), normed2, inverse2).astype(BF16)
    gnode[...] = mm_t(node2, p_out[...]).astype(BF16)

    def back2(rows):
        grad = mm(hot2[rows, mesh_rows:local2], gnode[...])
        gpre[rows, :] = (grad * slope2[rows, :]).astype(BF16)

    chunks(back2)
    mine = pl.ds(pl.multiple_of(core * half, COARSE), half)
    other = pl.ds(pl.multiple_of((1 - core) * half, COARSE), half)
    swap = remote(gcoarse.at[0], gcoarse.at[1], swap_sem.at[0], swap_sem.at[1], {"group": partner})
    hot2c = hot2t.at[local2:all2]
    gcoarse[0] = mm(hot2c[other, :], gpre[...]).astype(BF16)
    swap.start()
    gcoarse[2] = mm(hot2c[mine, :], gpre[...]).astype(BF16)
    g_local = mm(hot2t[0:mesh_rows, :], gpre[...]).astype(BF16)
    swap.wait()
    scatter = {}
    for k in far_first + [0]:
        to = level_at(k)
        rows = pl.ds(pl.multiple_of(to * COARSE, COARSE), COARSE)
        joint[k] = (gcoarse[2, rows, :].astype(F32) + gcoarse[1, rows, :].astype(F32)).astype(BF16)
        if k:
            scatter[k] = remote(
                joint.at[k],
                rs_buf.at[k - 1],
                rs_send.at[k - 1],
                rs_recv.at[k - 1],
                {"group": 2 * to + core},
            )
            scatter[k].start()
    g_dest = mm(hot2t[mesh_rows:local2, :], gpre[...]).astype(BF16)
    grad_up = cot + mm_t(g_local, p_src[...]) + mm_t(g_dest, p_dst[...])
    gup[...] = grad_up
    gain = e_gain_ref[...].reshape(1, -1)
    node1 = norm_backward(grad_up * gain, normed[...], inv[:, 0:1])
    row = lax.broadcasted_iota(jnp.int32, node1.shape, 0)
    node1 = jnp.where(row < COARSE, 0.0, node1).astype(BF16)
    gnode[...] = mm_t(node1, w_out[...]).astype(BF16)

    def early3(rows):
        acc[rows, :] = mm(hot1[rows, grid_rows:own1], gnode[...])

    chunks(early3)
    gnode16[...] = jnp.zeros_like(gnode16)
    for k in far_first:
        scatter[k].wait()

    total = joint[0].astype(F32)
    for k in range(levels - 1):
        total = total + rs_buf[k].astype(F32)
    high = total.astype(BF16)
    low = (total - high.astype(F32)).astype(BF16)
    both = mm_t(jnp.concatenate([high, low], axis=0), p_src[...])
    fixed = gup[0:COARSE, :] + both[0:COARSE, :] + both[COARSE:, :]
    gup[0:COARSE, :] = fixed
    node16 = norm_backward(fixed * gain, normed[0:COARSE, :], inv[0:COARSE, 0:1]).astype(BF16)
    gnode16[0:COARSE, :] = mm_t(node16, w_out[...]).astype(BF16)

    def late3(rows):
        grad = acc[rows, :] + mm(hot1[rows, grid_rows : grid_rows + LANES], gnode16[...])
        gpre[rows, :] = (grad * slope1[rows, :]).astype(BF16)

    chunks(late3)
    g_halo[...] = mm(hot1t[own1 : own1 + 2 * rim, :], gpre[...]).astype(BF16)
    back_up = remote(
        g_halo.at[rim : 2 * rim],
        peers.at[0:rim],
        back_send.at[0],
        back_recv.at[0],
        {"patch": after},
    )
    back_down = remote(
        g_halo.at[0:rim],
        peers.at[rim : 2 * rim],
        back_send.at[1],
        back_recv.at[1],
        {"patch": before},
    )
    back_up.start()
    back_down.start()
    g_own = mm(hot1t[0:grid_rows, :], gpre[...]).astype(BF16)
    own[...] = mm_t(g_own, w_src[...])
    g_targ = mm(hot1t[grid_rows:own1, :], gpre[...]).astype(BF16)
    mesh_out[...] = (gup[...] + mm_t(g_targ, w_dst[...])).astype(BF16)
    back_down.wait()
    returned = mm_t(peers[rim : 2 * rim, :], w_src[...]).astype(BF16)
    own[...] += mm(hot_ht[:, rim : 2 * rim], returned)
    back_up.wait()
    returned = mm_t(peers[0:rim, :], w_src[...]).astype(BF16)
    grid_out[...] = (own[...] + mm(hot_ht[:, 0:rim], returned)).astype(BF16)


def write_out(grid_ref, mesh_ref, grid_out, mesh_out, sem):
    copies = [
        pltpu.make_async_copy(grid_ref, grid_out, sem.at[0]),
        pltpu.make_async_copy(mesh_ref, mesh_out, sem.at[1]),
    ]
    for copy in copies:
        copy.start()
    for copy in copies:
        copy.wait()


def on_device(
    n_patch,
    n_group,
    grid_latent,
    mesh_latent,
    cotangent,
    halo_rows,
    encoder_sender,
    encoder_target,
    encoder_count,
    process_sender,
    process_target,
    process_count,
    encoder_source,
    encoder_dest,
    encoder_output,
    encoder_gain,
    process_source,
    process_dest,
    process_output,
    process_gain,
):
    g, d = grid_latent.shape
    m = mesh_latent.shape[0]
    h2 = halo_rows.shape[0]
    e = encoder_sender.shape[0]
    nc = n_group * COARSE
    hbm = pl.BlockSpec(memory_space=pltpu.MemorySpace.HBM)
    smem = pl.BlockSpec(memory_space=pltpu.SMEM)
    vmem = pl.BlockSpec(memory_space=pltpu.VMEM)
    dma = pltpu.SemaphoreType.DMA
    out = pl.pallas_call(
        functools.partial(kernel, n_patch, n_group),
        out_shape=(
            jax.ShapeDtypeStruct((g, d), BF16),
            jax.ShapeDtypeStruct((m, d), BF16),
        ),
        in_specs=[hbm] * 9 + [vmem] + [hbm] * 2 + [smem] + [hbm] * 2 + [smem] + [hbm] * 2,
        out_specs=(vmem, vmem),
        scratch_shapes=[
            pltpu.VMEM((g, d), BF16),
            pltpu.VMEM((h2, d), BF16),
            pltpu.VMEM((m, d), BF16),
            pltpu.VMEM((m, d), BF16),
        ]
        + [pltpu.VMEM((d, d), BF16)] * 6
        + [
            pltpu.VMEM((h2, d), BF16),
            pltpu.VMEM((h2, g), BF16),
            pltpu.VMEM((g, h2), BF16),
            pltpu.VMEM((e, g + m + h2), BF16),
            pltpu.VMEM((g + m + h2, e), BF16),
            pltpu.VMEM((e, 2 * m + nc), BF16),
            pltpu.VMEM((2 * m + nc, e), BF16),
            pltpu.VMEM((g + m, d), BF16),
            pltpu.VMEM((2 * m, d), BF16),
            pltpu.VMEM((nc, d), BF16),
            pltpu.VMEM((COARSE, d), BF16),
            pltpu.VMEM((e, d), F32),
            pltpu.VMEM((e, d), F32),
            pltpu.VMEM((e, d), F32),
            pltpu.VMEM((e, d), BF16),
            pltpu.VMEM((e, d), BF16),
            pltpu.VMEM((m, d), F32),
            pltpu.VMEM((m, LANES), F32),
            pltpu.VMEM((m, d), F32),
            pltpu.VMEM((m, d), BF16),
            pltpu.VMEM((LANES, d), BF16),
            pltpu.VMEM((3, nc // 2, d), BF16),
            pltpu.VMEM((n_group // 2, COARSE, d), BF16),
            pltpu.VMEM((n_group // 2 - 1, COARSE, d), BF16),
            pltpu.VMEM((h2, d), BF16),
            pltpu.VMEM((h2, d), BF16),
            pltpu.VMEM((g, d), F32),
            pltpu.VMEM((e,), jnp.int32),
            pltpu.VMEM((e,), jnp.int32),
            pltpu.VMEM((e,), jnp.int32),
            pltpu.VMEM((e,), jnp.int32),
            pltpu.VMEM((d,), F32),
            pltpu.VMEM((d,), F32),
            dma((4,)),
            dma((14,)),
            dma((2,)),
            dma((2,)),
            dma((n_group,)),
            dma((n_group,)),
            dma((2,)),
            dma((n_group // 2 - 1,)),
            dma((n_group // 2 - 1,)),
            dma((2,)),
            dma((2,)),
        ],
        compiler_params=pltpu.CompilerParams(
            collective_id=0, has_side_effects=True, vmem_limit_bytes=40 * 1024 * 1024
        ),
        name="step",
    )(
        *[
            x if n in (9, 12, 15) else pltpu.with_memory_space_constraint(x, pltpu.MemorySpace.HBM)
            for n, x in enumerate((
        grid_latent,
        mesh_latent,
        cotangent,
        encoder_source,
        encoder_dest,
        encoder_output,
        process_source,
        process_dest,
        process_output,
        halo_rows,
        encoder_sender,
        encoder_target,
        encoder_count,
        process_sender,
        process_target,
        process_count,
        encoder_gain,
        process_gain,
            ))
        ]
    )
    out = [pltpu.with_memory_space_constraint(x, pltpu.MemorySpace.VMEM) for x in out]
    return pl.pallas_call(
        write_out,
        out_shape=(jax.ShapeDtypeStruct((g, d), BF16), jax.ShapeDtypeStruct((m, d), BF16)),
        in_specs=[vmem, vmem],
        out_specs=(hbm, hbm),
        scratch_shapes=[dma((2,))],
        name="write_out",
    )(*out)


def solution(mesh):
    both = P(("patch", "group"))
    rows = P(("patch", "group"), None)
    return jax.shard_map(
        functools.partial(on_device, mesh.shape["patch"], mesh.shape["group"]),
        mesh=mesh,
        in_specs=(rows,) * 3 + (both,) * 7 + (P(),) * 8,
        out_specs=(rows, rows),
        check_vma=False,
    )
```

```python
import functools

import jax
import jax.numpy as jnp
from jax import lax
from jax.experimental import pallas as pl
from jax.experimental.pallas import tpu as pltpu
from jax.sharding import PartitionSpec as P

EPSILON = 1e-05
F32 = jnp.float32
BF16 = jnp.bfloat16
COARSE = 16
LANES = 128


def mm(a, b):
    return jnp.dot(a, b, preferred_element_type=F32)


def mm_t(a, b):
    return lax.dot_general(a, b, (((1,), (1,)), ((), ())), preferred_element_type=F32)


def column(row):
    return jnp.transpose(jnp.broadcast_to(row, (LANES, row.shape[1])))


def onehot_cols(ref, col, start, stop, shift):
    lane = lax.broadcasted_iota(jnp.int32, (col.shape[0], LANES), 1)
    for c in range(start, stop, LANES):
        width = min(LANES, stop - c)
        hit = jnp.where(col == lane + (c - shift), 1.0, 0.0).astype(BF16)
        ref[:, c : c + width] = hit[:, :width]


def onehot_rows(ref, row, start, stop, shift):
    for c in range(start, stop, LANES):
        height = min(LANES, stop - c)
        sub = lax.broadcasted_iota(jnp.int32, (height, row.shape[1]), 0)
        hit = jnp.where(row == sub + (c - shift), 1.0, 0.0).astype(BF16)
        ref[c : c + height, :] = hit


def norm_backward(scaled, normed, inverse):
    first = jnp.mean(scaled, axis=-1, keepdims=True)
    second = jnp.mean(scaled * normed, axis=-1, keepdims=True)
    return inverse * (scaled - first - normed * second)


def norm_forward(values):
    center = values - jnp.mean(values, axis=-1, keepdims=True)
    inverse = lax.rsqrt(jnp.mean(center * center, axis=-1, keepdims=True) + EPSILON)
    return center * inverse, inverse


def silu_pair(values):
    logistic = 0.5 * jnp.tanh(0.5 * values) + 0.5
    hidden = values * logistic
    return hidden, logistic + hidden * (1.0 - logistic)


def silu(values):
    return values * (0.5 * jnp.tanh(0.5 * values) + 0.5)


def kernel(
    n_patch,
    n_group,
    grid_hbm,
    mesh_hbm,
    cot_hbm,
    w_src_hbm,
    w_dst_hbm,
    w_out_hbm,
    p_src_hbm,
    p_dst_hbm,
    p_out_hbm,
    halo_ref,
    e_send_hbm,
    e_targ_hbm,
    e_count_ref,
    p_send_hbm,
    p_targ_hbm,
    p_count_ref,
    e_gain_hbm,
    p_gain_hbm,
    grid_out,
    mesh_out,
    grid_v,
    ext,
    mesh_v,
    cot_v,
    w_src,
    w_dst,
    w_out,
    p_src,
    p_dst,
    p_out,
    outgoing,
    hot_h,
    hot_ht,
    hot1,
    hot1t,
    hot2,
    hot2t,
    tbl1,
    tbl2,
    coarse,
    coarse16,
    acc,
    slope1,
    slope2,
    hid,
    gpre,
    normed,
    inv,
    gup,
    gnode,
    gnode16,
    gcoarse,
    joint,
    rs_buf,
    g_halo,
    peers,
    own,
    e_send_ref,
    e_targ_ref,
    p_send_ref,
    p_targ_ref,
    e_gain_ref,
    p_gain_ref,
    grid_sem,
    load_sem,
    halo_send,
    halo_recv,
    co_send,
    co_recv,
    swap_sem,
    rs_send,
    rs_recv,
    back_send,
    back_recv,
):
    patch, group = lax.axis_index("patch"), lax.axis_index("group")
    after = lax.rem(patch + 1, n_patch)
    before = lax.rem(patch + n_patch - 1, n_patch)
    grid_rows, mesh_rows = grid_v.shape[0], mesh_hbm.shape[0]
    rim = outgoing.shape[0] // 2
    slots = e_send_ref.shape[0]
    chunk = 256
    mesh_id = pl.DeviceIdType.MESH

    core, level = lax.rem(group, 2), group // 2
    levels = n_group // 2
    partner = group + 1 - 2 * core

    def level_at(k):
        return lax.rem(level + k, levels)

    far_first = sorted(range(1, levels), key=lambda k: -min(k, levels - k))
    contacts = [{"group": 2 * level_at(k) + core} for k in far_first]
    contacts += [{"patch": before}, {"patch": after}, {"group": partner}]
    barrier = pltpu.get_barrier_semaphore()
    for where in contacts:
        pl.semaphore_signal(barrier, inc=1, device_id=where, device_id_type=mesh_id)

    pairs = (
        (e_send_hbm, e_send_ref),
        (e_targ_hbm, e_targ_ref),
        (w_src_hbm, w_src),
        (mesh_hbm, mesh_v),
        (w_dst_hbm, w_dst),
        (p_send_hbm, p_send_ref),
        (p_targ_hbm, p_targ_ref),
        (e_gain_hbm, e_gain_ref),
        (p_gain_hbm, p_gain_ref),
        (w_out_hbm, w_out),
        (p_src_hbm, p_src),
        (p_dst_hbm, p_dst),
        (p_out_hbm, p_out),
        (cot_hbm, cot_v),
    )
    loads = [
        pltpu.make_async_copy(src, dst, load_sem.at[n]) for n, (src, dst) in enumerate(pairs)
    ]
    quarter = grid_rows // 4
    first = [
        pltpu.make_async_copy(
            grid_hbm.at[n * quarter : (n + 1) * quarter],
            grid_v.at[n * quarter : (n + 1) * quarter],
            grid_sem.at[n],
        )
        for n in range(4)
    ]
    for copy in first + [loads[2]]:
        copy.start()

    halo_row = halo_ref[...].reshape(1, 2 * rim)
    onehot_cols(hot_h, column(halo_row), 0, grid_rows, 0)
    for copy in first + [loads[2]]:
        copy.wait()
    tbl1[0:grid_rows, :] = mm(grid_v[...], w_src[...]).astype(BF16)
    outgoing[...] = mm(hot_h[...], tbl1[0:grid_rows, :]).astype(BF16)
    pl.semaphore_wait(barrier, len(contacts))

    def remote(src, dst, send, recv, where):
        return pltpu.make_async_remote_copy(
            src_ref=src,
            dst_ref=dst,
            send_sem=send,
            recv_sem=recv,
            device_id=where,
            device_id_type=mesh_id,
        )

    up = remote(
        outgoing.at[rim : 2 * rim],
        ext.at[0:rim],
        halo_send.at[0],
        halo_recv.at[0],
        {"patch": after},
    )
    down = remote(
        outgoing.at[0:rim],
        ext.at[rim : 2 * rim],
        halo_send.at[1],
        halo_recv.at[1],
        {"patch": before},
    )
    up.start()
    down.start()
    for copy in loads[:2] + loads[3:]:
        copy.start()

    slot = lax.broadcasted_iota(jnp.int32, (1, slots), 1)
    own1 = grid_rows + mesh_rows
    for n in (0, 1):
        loads[n].wait()
    sender = e_send_ref[...].reshape(1, slots)
    sender = jnp.where(sender >= grid_rows, sender + mesh_rows, sender)
    target = jnp.where(slot < e_count_ref[0], e_targ_ref[...].reshape(1, slots), -1)
    sender_col, target_col = column(sender), column(target)
    onehot_cols(hot1, sender_col, 0, grid_rows, 0)
    onehot_cols(hot1, target_col, grid_rows, own1, grid_rows)
    onehot_cols(hot1, sender_col, own1, own1 + 2 * rim, 0)
    loads[3].wait()
    loads[4].wait()
    tbl1[grid_rows:own1, :] = mm(mesh_v[...], w_dst[...]).astype(BF16)

    def chunks(body):
        for i in range(0, slots, chunk):
            body(slice(i, i + chunk))

    def early1(rows):
        acc[rows, :] = mm(hot1[rows, 0:own1], tbl1[0:own1, :])

    chunks(early1)
    onehot_rows(hot1t, sender, 0, grid_rows, 0)
    onehot_rows(hot1t, target, grid_rows, own1, grid_rows)
    onehot_rows(hot1t, sender, own1, own1 + 2 * rim, 0)
    for n in range(5, 9):
        loads[n].wait()
    p_sender = p_send_ref[...].reshape(1, slots)
    local2 = 2 * mesh_rows
    all2 = local2 + coarse.shape[0]
    half = coarse.shape[0] // 2
    row_c = p_sender - mesh_rows
    row_c = ((row_c >> 4) & 1) * half + (row_c >> 5) * COARSE + (row_c & 15)
    p_sender = jnp.where(p_sender >= mesh_rows, row_c + local2, p_sender)
    p_target = jnp.where(slot < p_count_ref[0], p_targ_ref[...].reshape(1, slots), -1)
    p_sender_col, p_target_col = column(p_sender), column(p_target)
    onehot_cols(hot2, p_sender_col, 0, mesh_rows, 0)
    onehot_cols(hot2, p_target_col, mesh_rows, local2, mesh_rows)
    onehot_cols(hot2, p_sender_col, local2, all2, 0)
    onehot_rows(hot2t, p_sender, 0, mesh_rows, 0)
    onehot_rows(hot2t, p_target, mesh_rows, local2, mesh_rows)
    onehot_rows(hot2t, p_sender, local2, all2, 0)
    onehot_rows(hot_ht, halo_row, 0, grid_rows, 0)

    up.wait()
    down.wait()
    def late1(rows):
        preact = acc[rows, :] + mm(hot1[rows, own1 : own1 + 2 * rim], ext[...])
        hid[rows, :] = silu(preact).astype(BF16)
        slope1[rows, :] = preact

    chunks(late1)
    for n in range(9, len(pairs)):
        loads[n].wait()
    summed16 = mm(hot1t[grid_rows : grid_rows + COARSE, :], hid[...]).astype(BF16)
    normed16 = norm_forward(mm(summed16, w_out[...]))[0]
    mesh16 = mesh_v[0:COARSE, :].astype(F32)
    updated16 = (mesh16 + normed16 * e_gain_ref[...].reshape(1, -1)).astype(BF16)
    coarse16[...] = mm(updated16, p_src[...]).astype(BF16)

    def rows_of(c, z):
        return pl.ds(pl.multiple_of(c * half + z * COARSE, COARSE), COARSE)

    own_rows = rows_of(core, level)
    give = remote(
        coarse16, coarse.at[own_rows], co_send.at[0], co_recv.at[0], {"group": partner}
    )
    spread, relay = {}, {}
    for k in far_first:
        spread[k] = remote(
            coarse16,
            coarse.at[own_rows],
            co_send.at[k],
            co_recv.at[k],
            {"group": 2 * level_at(k) + core},
        )
        got = rows_of(core, level_at(levels - k))
        relay[k] = remote(
            coarse.at[got],
            coarse.at[got],
            co_send.at[levels + k],
            co_recv.at[levels + k],
            {"group": partner},
        )
    for k in far_first:
        spread[k].start()
    give.start()
    coarse[own_rows, :] = coarse16[...]
    summed = mm(hot1t[grid_rows:own1, :], hid[...]).astype(BF16)
    normed1, inverse1 = norm_forward(mm(summed, w_out[...]))
    normed[...] = normed1
    inv[...] = jnp.broadcast_to(inverse1, inv.shape)
    updated = (mesh_v[...].astype(F32) + normed1 * e_gain_ref[...].reshape(1, -1)).astype(BF16)
    projected = mm(updated, p_src[...]).astype(BF16)
    tbl2[0:mesh_rows, :] = projected
    tbl2[mesh_rows:local2, :] = mm(updated, p_dst[...]).astype(BF16)

    def early2(rows):
        acc[rows, :] = mm(hot2[rows, 0:local2], tbl2[...])
        slope1[rows, :] = silu_pair(slope1[rows, :])[1]

    chunks(early2)
    for k in reversed(far_first):
        spread[k].wait_recv()
        relay[k].start()
    give.wait()
    for k in far_first:
        spread[k].wait_send()
    for k in reversed(far_first):
        relay[k].wait()

    def late2(rows):
        preact = acc[rows, :] + mm(hot2[rows, local2:all2], coarse[...])
        hidden, slope = silu_pair(preact)
        hid[rows, :] = hidden.astype(BF16)
        slope2[rows, :] = slope

    chunks(late2)
    summed2 = mm(hot2t[mesh_rows:local2, :], hid[...]).astype(BF16)
    normed2, inverse2 = norm_forward(mm(summed2, p_out[...]))
    cot = cot_v[...].astype(F32)
    node2 = norm_backward(cot * p_gain_ref[...].reshape(1, -1), normed2, inverse2).astype(BF16)
    gnode[...] = mm_t(node2, p_out[...]).astype(BF16)

    def back2(rows):
        grad = mm(hot2[rows, mesh_rows:local2], gnode[...])
        gpre[rows, :] = (grad * slope2[rows, :]).astype(BF16)

    chunks(back2)
    mine = pl.ds(pl.multiple_of(core * half, COARSE), half)
    other = pl.ds(pl.multiple_of((1 - core) * half, COARSE), half)
    swap = remote(gcoarse.at[0], gcoarse.at[1], swap_sem.at[0], swap_sem.at[1], {"group": partner})
    hot2c = hot2t.at[local2:all2]
    gcoarse[0] = mm(hot2c[other, :], gpre[...]).astype(BF16)
    swap.start()
    gcoarse[2] = mm(hot2c[mine, :], gpre[...]).astype(BF16)
    g_local = mm(hot2t[0:mesh_rows, :], gpre[...]).astype(BF16)
    swap.wait()
    scatter = {}
    for k in far_first + [0]:
        to = level_at(k)
        rows = pl.ds(pl.multiple_of(to * COARSE, COARSE), COARSE)
        joint[k] = (gcoarse[2, rows, :].astype(F32) + gcoarse[1, rows, :].astype(F32)).astype(BF16)
        if k:
            scatter[k] = remote(
                joint.at[k],
                rs_buf.at[k - 1],
                rs_send.at[k - 1],
                rs_recv.at[k - 1],
                {"group": 2 * to + core},
            )
            scatter[k].start()
    g_dest = mm(hot2t[mesh_rows:local2, :], gpre[...]).astype(BF16)
    grad_up = cot + mm_t(g_local, p_src[...]) + mm_t(g_dest, p_dst[...])
    gup[...] = grad_up
    gain = e_gain_ref[...].reshape(1, -1)
    node1 = norm_backward(grad_up * gain, normed[...], inv[:, 0:1])
    row = lax.broadcasted_iota(jnp.int32, node1.shape, 0)
    node1 = jnp.where(row < COARSE, 0.0, node1).astype(BF16)
    gnode[...] = mm_t(node1, w_out[...]).astype(BF16)

    def early3(rows):
        acc[rows, :] = mm(hot1[rows, grid_rows:own1], gnode[...])

    chunks(early3)
    gnode16[...] = jnp.zeros_like(gnode16)
    for k in far_first:
        scatter[k].wait()

    total = joint[0].astype(F32)
    for k in range(levels - 1):
        total = total + rs_buf[k].astype(F32)
    high = total.astype(BF16)
    low = (total - high.astype(F32)).astype(BF16)
    both = mm_t(jnp.concatenate([high, low], axis=0), p_src[...])
    fixed = gup[0:COARSE, :] + both[0:COARSE, :] + both[COARSE:, :]
    gup[0:COARSE, :] = fixed
    node16 = norm_backward(fixed * gain, normed[0:COARSE, :], inv[0:COARSE, 0:1]).astype(BF16)
    gnode16[0:COARSE, :] = mm_t(node16, w_out[...]).astype(BF16)

    def late3(rows):
        grad = acc[rows, :] + mm(hot1[rows, grid_rows : grid_rows + LANES], gnode16[...])
        gpre[rows, :] = (grad * slope1[rows, :]).astype(BF16)

    chunks(late3)
    g_halo[...] = mm(hot1t[own1 : own1 + 2 * rim, :], gpre[...]).astype(BF16)
    back_up = remote(
        g_halo.at[rim : 2 * rim],
        peers.at[0:rim],
        back_send.at[0],
        back_recv.at[0],
        {"patch": after},
    )
    back_down = remote(
        g_halo.at[0:rim],
        peers.at[rim : 2 * rim],
        back_send.at[1],
        back_recv.at[1],
        {"patch": before},
    )
    back_up.start()
    back_down.start()
    g_own = mm(hot1t[0:grid_rows, :], gpre[...]).astype(BF16)
    own[...] = mm_t(g_own, w_src[...])
    g_targ = mm(hot1t[grid_rows:own1, :], gpre[...]).astype(BF16)
    mesh_out[...] = (gup[...] + mm_t(g_targ, w_dst[...])).astype(BF16)
    back_down.wait()
    returned = mm_t(peers[rim : 2 * rim, :], w_src[...]).astype(BF16)
    own[...] += mm(hot_ht[:, rim : 2 * rim], returned)
    back_up.wait()
    returned = mm_t(peers[0:rim, :], w_src[...]).astype(BF16)
    grid_out[...] = (own[...] + mm(hot_ht[:, 0:rim], returned)).astype(BF16)


def write_out(grid_ref, mesh_ref, grid_out, mesh_out, sem):
    piece = 128
    copies = []
    for src, dst in ((grid_ref, grid_out), (mesh_ref, mesh_out)):
        for lo in range(0, src.shape[0], piece):
            rows = slice(lo, lo + piece)
            copies.append(pltpu.make_async_copy(src.at[rows], dst.at[rows], sem.at[len(copies)]))
    for copy in copies:
        copy.start()
    for copy in copies:
        copy.wait()


def on_device(
    n_patch,
    n_group,
    grid_latent,
    mesh_latent,
    cotangent,
    halo_rows,
    encoder_sender,
    encoder_target,
    encoder_count,
    process_sender,
    process_target,
    process_count,
    encoder_source,
    encoder_dest,
    encoder_output,
    encoder_gain,
    process_source,
    process_dest,
    process_output,
    process_gain,
):
    g, d = grid_latent.shape
    m = mesh_latent.shape[0]
    h2 = halo_rows.shape[0]
    e = encoder_sender.shape[0]
    nc = n_group * COARSE
    hbm = pl.BlockSpec(memory_space=pltpu.MemorySpace.HBM)
    smem = pl.BlockSpec(memory_space=pltpu.SMEM)
    vmem = pl.BlockSpec(memory_space=pltpu.VMEM)
    dma = pltpu.SemaphoreType.DMA
    out = pl.pallas_call(
        functools.partial(kernel, n_patch, n_group),
        out_shape=(
            jax.ShapeDtypeStruct((g, d), BF16),
            jax.ShapeDtypeStruct((m, d), BF16),
        ),
        in_specs=[hbm] * 9 + [vmem] + [hbm] * 2 + [smem] + [hbm] * 2 + [smem] + [hbm] * 2,
        out_specs=(vmem, vmem),
        scratch_shapes=[
            pltpu.VMEM((g, d), BF16),
            pltpu.VMEM((h2, d), BF16),
            pltpu.VMEM((m, d), BF16),
            pltpu.VMEM((m, d), BF16),
        ]
        + [pltpu.VMEM((d, d), BF16)] * 6
        + [
            pltpu.VMEM((h2, d), BF16),
            pltpu.VMEM((h2, g), BF16),
            pltpu.VMEM((g, h2), BF16),
            pltpu.VMEM((e, g + m + h2), BF16),
            pltpu.VMEM((g + m + h2, e), BF16),
            pltpu.VMEM((e, 2 * m + nc), BF16),
            pltpu.VMEM((2 * m + nc, e), BF16),
            pltpu.VMEM((g + m, d), BF16),
            pltpu.VMEM((2 * m, d), BF16),
            pltpu.VMEM((nc, d), BF16),
            pltpu.VMEM((COARSE, d), BF16),
            pltpu.VMEM((e, d), F32),
            pltpu.VMEM((e, d), F32),
            pltpu.VMEM((e, d), F32),
            pltpu.VMEM((e, d), BF16),
            pltpu.VMEM((e, d), BF16),
            pltpu.VMEM((m, d), F32),
            pltpu.VMEM((m, LANES), F32),
            pltpu.VMEM((m, d), F32),
            pltpu.VMEM((m, d), BF16),
            pltpu.VMEM((LANES, d), BF16),
            pltpu.VMEM((3, nc // 2, d), BF16),
            pltpu.VMEM((n_group // 2, COARSE, d), BF16),
            pltpu.VMEM((n_group // 2 - 1, COARSE, d), BF16),
            pltpu.VMEM((h2, d), BF16),
            pltpu.VMEM((h2, d), BF16),
            pltpu.VMEM((g, d), F32),
            pltpu.VMEM((e,), jnp.int32),
            pltpu.VMEM((e,), jnp.int32),
            pltpu.VMEM((e,), jnp.int32),
            pltpu.VMEM((e,), jnp.int32),
            pltpu.VMEM((d,), F32),
            pltpu.VMEM((d,), F32),
            dma((4,)),
            dma((14,)),
            dma((2,)),
            dma((2,)),
            dma((n_group,)),
            dma((n_group,)),
            dma((2,)),
            dma((n_group // 2 - 1,)),
            dma((n_group // 2 - 1,)),
            dma((2,)),
            dma((2,)),
        ],
        compiler_params=pltpu.CompilerParams(
            collective_id=0, has_side_effects=True, vmem_limit_bytes=40 * 1024 * 1024
        ),
        name="step",
    )(
        *[
            x if n in (9, 12, 15) else pltpu.with_memory_space_constraint(x, pltpu.MemorySpace.HBM)
            for n, x in enumerate((
        grid_latent,
        mesh_latent,
        cotangent,
        encoder_source,
        encoder_dest,
        encoder_output,
        process_source,
        process_dest,
        process_output,
        halo_rows,
        encoder_sender,
        encoder_target,
        encoder_count,
        process_sender,
        process_target,
        process_count,
        encoder_gain,
        process_gain,
            ))
        ]
    )
    out = [pltpu.with_memory_space_constraint(x, pltpu.MemorySpace.VMEM) for x in out]
    return pl.pallas_call(
        write_out,
        out_shape=(jax.ShapeDtypeStruct((g, d), BF16), jax.ShapeDtypeStruct((m, d), BF16)),
        in_specs=[vmem, vmem],
        out_specs=(hbm, hbm),
        scratch_shapes=[dma(((g + m) // 128,))],
        name="write_out",
    )(*out)


def solution(mesh):
    both = P(("patch", "group"))
    rows = P(("patch", "group"), None)
    return jax.shard_map(
        functools.partial(on_device, mesh.shape["patch"], mesh.shape["group"]),
        mesh=mesh,
        in_specs=(rows,) * 3 + (both,) * 7 + (P(),) * 8,
        out_specs=(rows, rows),
        check_vma=False,
    )
```
